32 devices in a mesh: replica: 2 (over y), section: 2 (over core), seq: 8 (over z, x).
Axes of the slice: x: 2, y: 2, z: 4, core: 2. Of those that a mesh axis runs over, the one named last changes fastest.
Arguments:
- latents: float32 [2, 1024, 64], P('section', ('replica', 'seq')), parts along dimension 1, may hold values from -6 to 6
- cond: bfloat16 [2, 3, 1024, 4096], P('section', None, ('replica', 'seq')), parts along dimension 2, may hold values from -60 to 60
- embed: bfloat16 [2, 3, 64, 4096], P('section'), may hold values from -0.75 to 0.75
- audio_table: bfloat16 [2, 64, 4096], P('section', 'replica'), parts along dimension 1, may hold values from -6 to 6
- audio_map: int32 [64], P(('replica', 'seq')), parts along dimension 0, may hold values from 0 to 31
- out_proj: bfloat16 [2, 4096, 64], P('section'), may hold values from -0.5 to 0.5
- tile_start: int32 [16], P('replica'), parts along dimension 0, may hold values 0 or 1
- conv_input: bfloat16 [3, 3, 16, 512], P(None, None, None, 'section'), may hold values from -0.5 to 0.5
- conv_first: bfloat16 [3, 3, 512, 512], P(None, None, None, 'section'), may hold values from -0.09375 to 0.09375
- conv_second_up: bfloat16 [3, 3, 512, 256], P(None, None, None, 'section'), may hold values from -0.09375 to 0.09375
- conv_second: bfloat16 [3, 3, 256, 256], P(None, None, None, 'section'), may hold values from -0.125 to 0.125
- conv_third_up: bfloat16 [3, 3, 256, 128], P(None, None, None, 'section'), may hold values from -0.125 to 0.125
- conv_third: bfloat16 [3, 3, 128, 128], P(None, None, None, 'section'), may hold values from -0.1875 to 0.1875
- conv_color: bfloat16 [3, 3, 128, 3], replicated, may hold values from -0.1875 to 0.1875
- gain_first: float32 [512], replicated, may hold values from 0.1 to 1.9
- gain_second: float32 [256], replicated, may hold values from 0.1 to 1.9
- gain_third: float32 [128], replicated, may hold values from 0.1 to 1.9
- gain_color: float32 [128], replicated, may hold values from 0.1 to 1.9
Outputs:
- handoff: float32 [2, 1024, 64], P('section', ('replica', 'seq')), parts along dimension 1
- image: float32 [3, 128, 512], P(None, ('replica', 'seq')), parts along dimension 1
The draws below stay inside these ranges and needn't reach their ends.
There are 2 independent parts, one for each index of `replica`. The reference program is written for one: setup_inputs(seed, part) draws one part's arguments, and reference() takes and returns one part's arrays. A program takes and returns all parts, laid end to end along the dimension named above; an argument that names none is the same for every part. Nothing has to cross between parts.
Inputs may be any that keep to these rules, and one draw needn't show every extreme that they name: `tile_start`: entry i is 1 where a decoder row tile begins at row block i; entry 0 is not read.
All inputs are finite; a program needn't handle non-finite values.
Results may differ from the reference program's by a relative error of at most 0.017.
Values may be sent and summed in bfloat16 or wider, within the bound.
A program may use at most 128 MiB of HBM per device.

```python
import math
import jax
import jax.numpy as jnp
from jax import lax

HEADS = 32
HSIZE = 128
HD = 4096
LCH = 16
PATCH = 64
TCOLS = 64
ROWS_DEV = 1
TOKENS = 512
SECTIONS = 2
AUDIO = 32
BLOCK = 16
BLOCKS = 32
TILES = 8
C1 = 512
C2 = 256
C3 = 128
RGB = 3
LROWS = 16
LCOLS = 128


def draw_cond(key, part):
    entries = jnp.clip(jax.random.normal(key, (SECTIONS, 3, TOKENS, HD), jnp.float32), -6.0, 6.0)
    return entries.astype(jnp.bfloat16)


def touch_ends(drawn, stream_key, low, top_value):
    longest = drawn.shape.index(max(drawn.shape))
    spots = []
    for shift in (0, 1):
        where = [jax.random.randint(jax.random.fold_in(stream_key, axis), (), 0, length) for axis, length in enumerate(drawn.shape)]
        where[longest] = (where[longest] + shift) % drawn.shape[longest]
        spots.append(tuple(where))
    return drawn.at[spots[0]].set(low).at[spots[1]].set(top_value)


def block_levels(own_key, shape, pieces, low, largest):
    loudness, own = 1.0, jax.random.fold_in(own_key, 6)
    for dim, shards_of in pieces:
        heights = jnp.exp(jax.random.uniform(jax.random.fold_in(own, dim), (shards_of,), jnp.float32, low / len(pieces), largest / len(pieces)))
        loudness = loudness * jnp.repeat(heights, shape[dim] // shards_of).reshape([-1 if axis == dim else 1 for axis in range(len(shape))])
    return loudness


def normal_values(rng, shape, scale, most, split=(), held_as=jnp.bfloat16):
    array = scale * jax.random.normal(rng, shape, jnp.float32)
    if split:
        array = array * block_levels(rng, shape, split, -0.22, 0.18)
    return jnp.clip(array, -most, most).astype(held_as)


def setup_inputs(seed: int = 0, part: int = 0) -> dict:
    arg_keys = jax.random.split(jax.random.key(seed), 19)
    part_keys = jax.random.split(jax.random.fold_in(arg_keys[18], part), 19)
    return {
        "latents": normal_values(part_keys[0], (SECTIONS, TOKENS, PATCH), 1.0, 6.0, ((0, 2), (1, 8)), jnp.float32),
        "cond": draw_cond(jax.random.fold_in(jax.random.fold_in(arg_keys[18], part), 71), part),
        "embed": normal_values(arg_keys[2], (SECTIONS, 3, PATCH, HD), PATCH ** -0.5, 0.75, ((0, 2),)),
        "audio_table": normal_values(part_keys[3], (SECTIONS, AUDIO, HD), 1.0, 6.0, ((0, 2),)),
        "audio_map": touch_ends(jax.random.randint(part_keys[4], (BLOCKS,), 0, AUDIO), jax.random.fold_in(part_keys[4], 1), 0, AUDIO - 1).astype(jnp.int32),
        "out_proj": normal_values(arg_keys[5], (SECTIONS, HD, PATCH), HSIZE ** -0.5, 0.5, ((0, 2),)),
        "tile_start": touch_ends((jax.random.randint(part_keys[6], (TILES,), 0, 4) < 1).astype(jnp.int32), jax.random.fold_in(part_keys[6], 1), 0, 1),
        "conv_input": normal_values(arg_keys[7], (3, 3, LCH, C1), (9 * LCH) ** -0.5, 0.5, ((3, 2),)),
        "conv_first": normal_values(arg_keys[8], (3, 3, C1, C1), (9 * C1) ** -0.5, 0.09375, ((3, 2),)),
        "conv_second_up": normal_values(arg_keys[9], (3, 3, C1, C2), (9 * C1) ** -0.5, 0.09375, ((3, 2),)),
        "conv_second": normal_values(arg_keys[10], (3, 3, C2, C2), (9 * C2) ** -0.5, 0.125, ((3, 2),)),
        "conv_third_up": normal_values(arg_keys[11], (3, 3, C2, C3), (9 * C2) ** -0.5, 0.125, ((3, 2),)),
        "conv_third": normal_values(arg_keys[12], (3, 3, C3, C3), (9 * C3) ** -0.5, 0.1875, ((3, 2),)),
        "conv_color": normal_values(arg_keys[13], (3, 3, C3, RGB), (9 * C3) ** -0.5, 0.1875),
        "gain_first": jnp.clip(1.0 + 0.18 * jax.random.normal(arg_keys[14], (C1,), jnp.float32), 0.1, 1.9),
        "gain_second": jnp.clip(1.0 + 0.18 * jax.random.normal(arg_keys[15], (C2,), jnp.float32), 0.1, 1.9),
        "gain_third": jnp.clip(1.0 + 0.18 * jax.random.normal(arg_keys[16], (C3,), jnp.float32), 0.1, 1.9),
        "gain_color": jnp.clip(1.0 + 0.18 * jax.random.normal(arg_keys[17], (C3,), jnp.float32), 0.1, 1.9),
    }


step_size = -0.5
norm_eps = 1e-06

def activate(field, gain):
    values = field.astype(jnp.float32)
    square_mean = lax.optimization_barrier(jnp.mean(values * values, axis=-1, keepdims=True))
    scaled = values * lax.rsqrt(square_mean + norm_eps) * gain
    return jax.nn.silu(scaled).astype(jnp.bfloat16)

def upsample(field):
    return jnp.repeat(jnp.repeat(field, 2, axis=0), 2, axis=1)

def tiled_conv(field, weight, tile_rows):
    height = field.shape[0]
    cols = field.shape[1]
    zero_row = jnp.zeros_like(field[:1])
    padded = jnp.concatenate([zero_row, field, zero_row], axis=0)
    zero_col = jnp.zeros_like(padded[:, :1])
    padded = jnp.concatenate([zero_col, padded, zero_col], axis=1)
    edge_tiles = jnp.concatenate([jnp.full((1,), -1, jnp.int32), tile_rows.astype(jnp.int32), jnp.full((1,), -2, jnp.int32)])
    result = jnp.zeros((height, cols, weight.shape[3]), jnp.float32)
    for row_tap in range(3):
        same_tile = (edge_tiles[row_tap:row_tap + height] == tile_rows).astype(field.dtype)
        for col_tap in range(3):
            window = padded[row_tap:row_tap + height, col_tap:col_tap + cols] * same_tile[:, None, None]
            product = jnp.dot(window.reshape(height * cols, -1), weight[row_tap, col_tap], preferred_element_type=jnp.float32)
            result = result + product.reshape(height, cols, -1)
    return result

def head_attention(trio):
    queries, key_rows, value_rows = trio
    scores = jnp.dot(queries, key_rows.T, preferred_element_type=jnp.float32) * (1.0 / math.sqrt(HSIZE))
    row_max = lax.optimization_barrier(jnp.max(scores, axis=1, keepdims=True))
    weights = jnp.exp(scores - row_max)
    denominator = lax.optimization_barrier(jnp.sum(weights, axis=1, keepdims=True))
    attended = jnp.dot(weights.astype(jnp.bfloat16), value_rows, preferred_element_type=jnp.float32) / denominator
    return attended.astype(jnp.bfloat16)

def split_heads(field):
    return field.reshape(TOKENS, HEADS, HSIZE).transpose(1, 0, 2)

def section_step(latent, cond_section, embed_section, table_section, frames, out_section):
    low = latent.astype(jnp.bfloat16)
    projected = jnp.einsum('tp,cph->cth', low.astype(jnp.float32), embed_section.astype(jnp.float32))
    audio = table_section[frames].astype(jnp.float32)
    queries = (projected[0] + cond_section[0].astype(jnp.float32) + audio).astype(jnp.bfloat16)
    key_rows = (projected[1] + cond_section[1].astype(jnp.float32)).astype(jnp.bfloat16)
    value_rows = (projected[2] + cond_section[2].astype(jnp.float32) + audio).astype(jnp.bfloat16)
    attended = lax.map(head_attention, (split_heads(queries), split_heads(key_rows), split_heads(value_rows)))
    mixed = attended.transpose(1, 0, 2).reshape(TOKENS, HEADS * HSIZE)
    velocity = jnp.dot(mixed, out_section, preferred_element_type=jnp.float32)
    return latent + step_size * velocity

def reference(latents, cond, embed, audio_table, audio_map, out_proj, tile_start, conv_input, conv_first, conv_second_up, conv_second, conv_third_up, conv_third, conv_color, gain_first, gain_second, gain_third, gain_color):
    frames = audio_map[jnp.arange(TOKENS, dtype=jnp.int32) // BLOCK]
    outcomes = []
    for section_index in range(SECTIONS):
        outcomes.append(section_step(latents[section_index], cond[section_index], embed[section_index], audio_table[section_index], frames, out_proj[section_index]))
    outcome = jnp.stack(outcomes)
    handoff = jnp.roll(outcome, 1, axis=0)
    final = outcome[SECTIONS - 1]
    grid = final.reshape(LROWS // 2, TCOLS, 2, 2, LCH).transpose(0, 2, 1, 3, 4).reshape(LROWS, LCOLS, LCH).astype(jnp.bfloat16)
    tiles = jnp.cumsum(tile_start).astype(jnp.int32)
    block_rows = 2 * ROWS_DEV
    tile_one = tiles[jnp.arange(LROWS, dtype=jnp.int32) // block_rows]
    tile_two = tiles[jnp.arange(2 * LROWS, dtype=jnp.int32) // (2 * block_rows)]
    tile_three = tiles[jnp.arange(4 * LROWS, dtype=jnp.int32) // (4 * block_rows)]
    first_a = tiled_conv(grid, conv_input, tile_one).astype(jnp.bfloat16)
    first_b = (first_a.astype(jnp.float32) + tiled_conv(activate(first_a, gain_first), conv_first, tile_one)).astype(jnp.bfloat16)
    second_a = tiled_conv(upsample(first_b), conv_second_up, tile_two).astype(jnp.bfloat16)
    second_b = (second_a.astype(jnp.float32) + tiled_conv(activate(second_a, gain_second), conv_second, tile_two)).astype(jnp.bfloat16)
    third_a = tiled_conv(upsample(second_b), conv_third_up, tile_three).astype(jnp.bfloat16)
    third_b = (third_a.astype(jnp.float32) + tiled_conv(activate(third_a, gain_third), conv_third, tile_three)).astype(jnp.bfloat16)
    colors = tiled_conv(activate(third_b, gain_color), conv_color, tile_three)
    return (handoff, colors.transpose(2, 0, 1))
```

```python
import functools
import math

import jax
import jax.numpy as jnp
from jax import lax
from jax.experimental import pallas as pl
from jax.experimental.pallas import tpu as pltpu
from jax.sharding import PartitionSpec as P

HEADS = 32
HSIZE = 128


step_size = -0.5
norm_eps = 1e-06


MESH = pl.DeviceIdType.MESH
F32, BF16 = jnp.float32, jnp.bfloat16
NT = (((1,), (1,)), ((), ()))


def lanes_of(shape):
    return lax.broadcasted_iota(jnp.int32, shape, len(shape) - 1)


def rows_of(shape):
    return lax.broadcasted_iota(jnp.int32, shape, len(shape) - 2)


def swap_halves(value):
    return pltpu.roll(value, value.shape[1] // 2, 1)


def dot(x, w):
    return jnp.dot(x, w, preferred_element_type=F32)


def scaled(value, factor):
    return value * lax.broadcast(factor, value.shape).astype(BF16)


def pairs(x, y, z):
    return ((x, y + z), (x + y, z))


def lift_second(raw, lifted):
    depth = raw.shape[1]
    chunk = 64

    @pl.loop(0, depth // chunk)
    def _(i):
        row = pl.multiple_of(i * chunk, chunk)
        w = [raw[t, pl.ds(row, chunk)].astype(F32) for t in range(9)]
        by_row = [pairs(w[q], w[3 + q], w[6 + q]) for q in range(3)]
        for a in (0, 1):
            for p in (0, 1):
                cols = pairs(*(by_row[q][a][p] for q in range(3)))
                for b in (0, 1):
                    for q in (0, 1):
                        at = pl.multiple_of((2 * p + q) * depth + row, chunk)
                        lifted[2 * a + b, pl.ds(at, chunk)] = cols[b][q].astype(BF16)


def lift_third_up(raw, lifted):
    outs, depth = raw.shape[1:]
    zero = jnp.zeros((depth, outs), BF16)
    w = [raw[t].astype(F32) for t in range(9)]
    by_row = [pairs(w[q], w[3 + q], w[6 + q]) for q in range(3)]
    for a in (0, 1):
        for p in (0, 1):
            cols = pairs(*(by_row[q][a][p] for q in range(3)))
            for b in (0, 1):
                for at in range(3):
                    inside = 0 <= at - b <= 1
                    block = cols[b][at - b].T.astype(BF16) if inside else zero
                    row = (3 * p + at) * depth
                    lifted[a, row : row + depth, b * outs : (b + 1) * outs] = block


def lift_third(raw, lifted):
    outs, depth = raw.shape[1:]
    zero = jnp.zeros((depth, outs), BF16)
    for r in range(3):
        for at in range(4):
            for e in (0, 1):
                inside = 0 <= at - e <= 2
                block = raw[3 * r + at - e].astype(F32).T.astype(BF16) if inside else zero
                row = (4 * r + at) * depth
                lifted[row : row + depth, e * outs : (e + 1) * outs] = block


def lift_input(raw, lifted, cell):
    chans = cell // 4
    zero = jnp.zeros((chans, raw.shape[1]), BF16)
    for a in (0, 1):
        for b in (0, 1):
            blocks = []
            for p in (0, 1):
                for q in (0, 1):
                    for i in (0, 1):
                        for j in (0, 1):
                            u, v = 2 * p + i - 1 + a, 2 * q + j - 1 + b
                            inside = 0 <= u <= 2 and 0 <= v <= 2
                            row = (3 * u + v) * chans
                            blocks.append(raw[row : row + chans] if inside else zero)
            lifted[2 * a + b] = jnp.concatenate(blocks, axis=0)


def lift_color(raw, lifted):
    color = raw[...].astype(F32)
    color = jnp.concatenate([color, jnp.zeros((8 - color.shape[0], color.shape[1]), F32)], axis=0)
    depth = color.shape[1] // 9
    zero = jnp.zeros((8, depth), F32)
    tile = lambda t: color[:, t * depth : (t + 1) * depth]
    for pair in range(4):
        blocks = []
        for f in (2 * pair, 2 * pair + 1):
            blocks.append(
                jnp.concatenate(
                    [
                        tile(3 * r + at - f) if 0 <= at - f <= 2 else zero
                        for r in range(3)
                        for at in range(10)
                    ],
                    axis=1,
                )
            )
        lifted[16 * pair : 16 * (pair + 1)] = jnp.concatenate(blocks, axis=0).astype(BF16)


def step_kernel(
    splits, per, chunk, sections, devices,
    amap, starts,
    latent, cond, embed, table, out_t,
    c_in, c_first, c_up2, c_second, c_up3, c_third, c_color, gain1, gain2, gain3, gain4,
    handed, image,
    lat, latd, xcat, condv, eq, ek, ev, wt, sq, skv, gq, gkv, acc, part, parts, resd, result,
    low, tokens, keep,
    r_in, w_first, r_up2, w_second, r_up3, r_third, r_color, g1, g2, g3, g4,
    w_in, w_up2, w_up3, w_third, w_color, order,
    a1, p1, x1, a2, p2, x2, a3, p3, p4, picture,
    in_sem, send_q, recv_q, send_kv, recv_kv, own_sem, send_p, recv_p,
    here_sem, send_w, recv_w, send_h, recv_h, send_r, recv_r, send_i, recv_i, out_sem, go,
):
    me = lax.axis_index("seq")
    section = lax.axis_index("section")
    last = section == sections - 1
    partner = {"section": lax.rem(section + 1, sections)}
    groups = devices // splits
    count, patch = lat.shape
    half = count // splits
    wide = chunk * HSIZE
    chunks = per // chunk
    my_group = me // splits
    cols = count

    tokens[...] = jnp.zeros(tokens.shape, BF16)
    barrier = pltpu.get_barrier_semaphore()
    for t in range(sections):

        @pl.loop(0, devices)
        def _(d):
            @pl.when(jnp.logical_or(d != me, section != t))
            def _():
                pl.semaphore_signal(
                    barrier, inc=1, device_id={"section": t, "seq": d}, device_id_type=MESH
                )

    frames = table.shape[0]
    loads = [
        pltpu.make_async_copy(src, dst, in_sem.at[k])
        for k, (src, dst) in enumerate(
            (
                (latent, lat), (embed.at[0], eq.at[pl.ds(0, patch)]),
                (table, eq.at[pl.ds(patch, frames)]), (embed.at[2], ev.at[pl.ds(0, patch)]),
                (table, ev.at[pl.ds(patch, frames)]), (embed.at[1], ek), (cond, condv),
                (out_t, wt), (gain1, g1), (gain2, g2), (gain3, g3), (gain4, g4),
                (c_color, r_color),
            )
        )
    ]
    for copy in loads:
        copy.start()

    weights = ((c_third, r_third), (c_in, r_in), (c_up3, r_up3), (c_up2, r_up2),
               (c_first, w_first), (c_second, w_second))

    def half_of(dst, k):
        if k in (0, 2):
            size = dst.shape[1] // 2
            return dst.at[:, pl.ds(pl.multiple_of(section * size, size), size)]
        size = dst.shape[-1] // 2
        lanes = pl.ds(pl.multiple_of(section * size, size), size)
        return dst.at[:, :, lanes] if len(dst.shape) == 3 else dst.at[:, lanes]

    mine = [
        pltpu.make_async_copy(src, half_of(dst, k), here_sem.at[k])
        for k, (src, dst) in enumerate(weights)
    ]
    given_w = [
        pltpu.make_async_remote_copy(
            src_ref=src, dst_ref=half_of(dst, k), send_sem=send_w.at[k], recv_sem=recv_w.at[k],
            device_id=partner, device_id_type=MESH,
        )
        for k, (src, dst) in enumerate(weights)
    ]

    blocks = starts.shape[0]

    def joined(by):
        block = me + by
        inside = jnp.logical_and(block >= 0, block + 1 < blocks)
        begins = starts[jnp.clip(block + 1, 0, blocks - 1)]
        return jnp.where(jnp.logical_and(inside, begins == 0), 1.0, 0.0).astype(F32)

    k_a, k_b, k_c, k_d = (joined(by) for by in (-2, -1, 0, 1))
    one = jnp.float32(1.0)
    upper = section == 0
    either = lambda x, y: jnp.where(upper, x, y)
    level1 = [either(x, y) for x, y in (
        (k_a, one), (one, k_b), (k_b, one), (one, k_c), (k_c, one), (one, k_d))]
    level2 = [either(x, y) for x, y in ((one, k_b), (k_b, one), (one, k_c), (k_c, one))]
    b_or, c_or = either(k_b, one), either(one, k_c)
    for k, value in enumerate(
        [k_a, k_b, k_c, k_d] + level1 + level2 + [one, b_or, one, c_or, one, one, one]
        + [b_or, one, c_or]
    ):
        keep[k] = value

    zrow = patch + frames
    eq[zrow:] = jnp.zeros((eq.shape[0] - zrow, eq.shape[1]), BF16)
    ev[zrow:] = jnp.zeros((ev.shape[0] - zrow, ev.shape[1]), BF16)
    perm_row = rows_of(order.shape)
    perm_col = lanes_of(order.shape)
    phase = lax.div(perm_row, jnp.int32(cols))
    target = (perm_row - phase * cols) * 8 + phase
    order[...] = jnp.where(perm_col == target, 1.0, 0.0).astype(BF16)

    loads[0].wait()
    latd[:, :patch] = lat[...]
    latd[:, patch:] = lat[...]
    row = rows_of(xcat.shape)
    lane = lanes_of(xcat.shape)
    per_block = count // amap.shape[0]
    frame = lax.broadcast(amap[0], xcat.shape)
    for k in range(1, amap.shape[0]):
        frame = jnp.where(row >= k * per_block, amap[k], frame)
    padded = latd[...]
    if xcat.shape[1] > padded.shape[1]:
        extra = xcat.shape[1] - padded.shape[1]
        padded = jnp.concatenate([padded, jnp.zeros((count, extra), F32)], axis=1)
    onehot = jnp.where(lane == frame + patch, 1.0, 0.0)
    xcat[...] = jnp.where(lane < patch, padded, onehot).astype(BF16)
    for copy in loads[1:8]:
        copy.wait()

    def q_copy(c, d, src):
        return pltpu.make_async_remote_copy(
            src_ref=sq.at[d // splits, c, pl.ds(lax.rem(d, splits) * half, half)],
            dst_ref=gq.at[c, pl.ds(src * half, half)],
            send_sem=send_q.at[c, d], recv_sem=recv_q.at[c, src],
            device_id={"seq": d}, device_id_type=MESH,
        )

    def kv_copy(c, d, src):
        return pltpu.make_async_remote_copy(
            src_ref=skv.at[d // splits, c],
            dst_ref=gkv.at[c, pl.ds(src * count, count)],
            send_sem=send_kv.at[c, d], recv_sem=recv_kv.at[c, src],
            device_id={"seq": d}, device_id_type=MESH,
        )

    near = max(groups // 2, 1)

    def turn(k):
        side = lax.rem(my_group // near + 1 + k // near, max(groups // near, 1))
        return side * near + lax.rem(my_group + 1 + lax.rem(k, near), near)

    def send(c, g):
        @pl.loop(0, splits)
        def _(r):
            d = g * splits + r

            @pl.when(d != me)
            def _():
                q_copy(c, d, me).start()
                kv_copy(c, d, me).start()

    pl.semaphore_wait(barrier, sections * devices - 1)
    for copy in given_w[:2]:
        copy.start()
    for copy in mine:
        copy.start()

    for c in range(chunks):

        @pl.loop(0, groups)
        def _(k):
            g = turn(k)
            at = pl.ds(pl.multiple_of(g * (per * HSIZE) + c * wide, HSIZE), wide)
            q = dot(xcat[...], eq[:, at]) + condv[0, :, at].astype(F32)
            key = dot(xcat[:, :patch], ek[:, at]) + condv[1, :, at].astype(F32)
            v = dot(xcat[...], ev[:, at]) + condv[2, :, at].astype(F32)
            w = wt[:, at]
            if chunk == 2:
                first = lanes_of(w.shape) < HSIZE
                zero = jnp.zeros(w.shape, BF16)
                w = jnp.concatenate([jnp.where(first, w, zero), jnp.where(first, zero, w)], axis=0)
            else:
                w = jnp.concatenate([w, jnp.zeros((128 - w.shape[0], w.shape[1]), BF16)], axis=0)
            mixed = lax.dot_general(v.astype(BF16), w, NT, preferred_element_type=F32)
            sq[g, c] = q.astype(BF16)
            skv[g, c, :, :wide] = key.astype(BF16)
            skv[g, c, :, wide:] = mixed.astype(BF16)

            @pl.when(last)
            def _():
                send(c, g)

    for copy in given_w[2:]:
        copy.start()

    own = []
    for c in range(chunks):
        own.append(pltpu.make_async_copy(
            sq.at[my_group, c, pl.ds(lax.rem(me, splits) * half, half)],
            gq.at[c, pl.ds(me * half, half)], own_sem.at[c, 0],
        ))
        own.append(pltpu.make_async_copy(
            skv.at[my_group, c], gkv.at[c, pl.ds(me * count, count)], own_sem.at[c, 1]
        ))
    for copy in own:
        copy.start()

    for copy in loads[8:]:
        copy.wait()
    lift_color(r_color, w_color)
    mine[0].wait()
    given_w[0].wait_recv()
    lift_third(r_third, w_third)
    mine[1].wait()
    given_w[1].wait_recv()
    lift_input(r_in, w_in, patch)
    mine[2].wait()
    given_w[2].wait_recv()
    lift_third_up(r_up3, w_up3)
    mine[3].wait()
    given_w[3].wait_recv()
    lift_second(r_up2, w_up2)

    queries = gq.shape[1]
    block = min(256, queries)
    parts_of = queries // block
    scale = 1.0 / math.sqrt(HSIZE)
    lane128 = lanes_of((block, 128))
    both = half // 2

    def attend(c):
        own[2 * c].wait()
        own[2 * c + 1].wait()

        @pl.loop(0, devices)
        def _(d):
            @pl.when(d != me)
            def _():
                q_copy(c, d, d).wait_recv()
                kv_copy(c, d, d).wait_recv()

        @pl.loop(0, parts_of)
        def _(i):
            at = pl.ds(pl.multiple_of(i * block, block), block)
            outs = []
            for h in range(chunk):
                own_lanes = slice(h * HSIZE, (h + 1) * HSIZE)
                scores = lax.dot_general(
                    gq[c, at, own_lanes], gkv[c, :, own_lanes], NT, preferred_element_type=F32
                ) * scale
                top = jnp.max(scores, axis=1, keepdims=True)
                weights_h = jnp.exp(scores - top)
                total = jnp.sum(weights_h, axis=1, keepdims=True)
                outs.append(dot(weights_h.astype(BF16), gkv[c, :, wide:]) / total)
            value = outs[0] if chunk == 1 else jnp.where(lane128 < patch, outs[0], outs[1])
            if c > 0:
                value = value + acc[at]
            if c < chunks - 1:
                acc[at] = value
            else:
                value = value + swap_halves(value)
                for k in range(block // half):
                    low_rows = value[k * half : k * half + both]
                    high_rows = value[k * half + both : (k + 1) * half]
                    first = lanes_of(low_rows.shape) < patch
                    part[i * (block // half) + k] = jnp.where(first, low_rows, high_rows)

    def part_copy(d, src):
        return pltpu.make_async_remote_copy(
            src_ref=part.at[d], dst_ref=parts.at[src],
            send_sem=send_p.at[d], recv_sem=recv_p.at[src],
            device_id={"seq": d}, device_id_type=MESH,
        )

    def send_parts():
        @pl.loop(1, devices)
        def _(k):
            part_copy(lax.rem(me + k, devices), me).start()

    def settle():
        @pl.loop(0, devices)
        def _(d):
            @pl.when(d != me)
            def _():
                part_copy(d, d).wait_recv()

        for r in range(splits):
            total = jnp.zeros((both, 128), F32)
            for g in range(groups):
                d = g * splits + r
                total = total + jnp.where(d == me, part[d], parts[d])
            first = lanes_of(total.shape) < patch
            other = swap_halves(total)
            at = r * half
            low_rows = jnp.where(first, total, other)
            high_rows = jnp.where(first, other, total)
            resd[at : at + both] = latd[at : at + both] + step_size * low_rows
            resd[at + both : at + half] = latd[at + both : at + half] + step_size * high_rows
        result[...] = resd[:, :patch]

    given = pltpu.make_async_remote_copy(
        src_ref=result, dst_ref=handed, send_sem=send_r, recv_sem=recv_r,
        device_id=partner, device_id_type=MESH,
    )

    def row_copy(by, t, to):
        return pltpu.make_async_remote_copy(
            src_ref=low, dst_ref=tokens.at[2 - by],
            send_sem=send_h.at[2 - by, t], recv_sem=recv_h.at[2 - by],
            device_id={"section": t, "seq": lax.rem(to + devices, devices)}, device_id_type=MESH,
        )

    side_copy = pltpu.make_async_remote_copy(
        src_ref=low, dst_ref=tokens.at[2], send_sem=send_h.at[2, 0], recv_sem=recv_h.at[2],
        device_id=partner, device_id_type=MESH,
    )

    def inside(by):
        return jnp.logical_and(me + by >= 0, me + by < devices)

    def sent_all():
        @pl.loop(0, devices)
        def _(d):
            @pl.when(d != me)
            def _():
                for c in range(chunks):
                    q_copy(c, d, me).wait_send()
                    kv_copy(c, d, me).wait_send()

    @pl.when(last)
    def _():
        for c in range(chunks):
            if c == chunks - 1:
                sent_all()
                pl.semaphore_signal(go, inc=1, device_id=partner, device_id_type=MESH)
            attend(c)
        send_parts()
        settle()
        low[...] = resd[...].astype(BF16)
        for by in (1, -1, 2, -2):
            for t in range(sections):

                @pl.when(inside(by))
                def _():
                    row_copy(by, t, me + by).start()

        side_copy.start()
        given.start()
        tokens[2] = low[...]

    @pl.when(jnp.logical_not(last))
    def _():
        pl.semaphore_wait(go, 1)
        for c in range(chunks):

            @pl.loop(0, groups)
            def _(k):
                send(c, turn(k))

        side_copy.wait_recv()

    for by in (1, -1, 2, -2):

        @pl.when(inside(-by))
        def _():
            row_copy(by, 0, me - by).wait_recv()

    def moved(value, by):
        position = rows_of(value.shape)
        if by > 0:
            return jnp.where(position > 0, pltpu.roll(value, 1, 0), 0.0)
        return jnp.where(position < cols - 1, pltpu.roll(value, cols - 1, 0), 0.0)

    def put(buf, index, value):
        phases = value.shape[0]
        buf[index, 1 : phases + 1] = value.astype(BF16)
        buf[index, 0] = moved(value[phases - 1], 1).astype(BF16)
        buf[index, phases + 1] = moved(value[0], -1).astype(BF16)

    def act(value, gain):
        square = jnp.mean(value * value, axis=-1, keepdims=True)
        h = value * (0.5 * lax.rsqrt(square + norm_eps)) * gain[...]
        return h + h * jnp.tanh(h)

    def flat(value):
        return value.reshape(-1, value.shape[-1])

    cells = []
    for i in range(5):
        value = tokens[i].astype(F32)
        first = lanes_of(value.shape) < patch
        cells.append((
            jnp.where(first, moved(value, 1), value).astype(BF16),
            jnp.where(first, value, moved(value, -1)).astype(BF16),
        ))
    for a in (0, 1):
        for b in (0, 1):
            x = []
            for j in range(4):
                above, below = cells[j][b], cells[j + 1][b]
                if a == 0:
                    above = scaled(above, keep[j])
                else:
                    below = scaled(below, keep[j])
                x.append(jnp.concatenate([above, below], axis=1))
            y = dot(jnp.concatenate(x, axis=0), w_in[2 * a + b]).astype(BF16)
            for j in range(4):
                a1[2 * j + 1 - a, b] = y[j * cols : (j + 1) * cols]

    shift = section

    @pl.loop(0, 7)
    def _(i):
        put(p1, i, act(a1[i + shift].astype(F32), g1))

    mine[4].wait()
    given_w[4].wait_recv()
    outs1 = w_first.shape[1] // 2
    for n in range(2):
        taps = []
        for p in range(3):
            for q in range(3):
                piece = []
                for j in range(5):
                    value = p1[j + p, q : q + 2]
                    if p == 0:
                        value = scaled(value, keep[4 + j])
                    elif p == 2:
                        value = scaled(value, keep[5 + j])
                    piece.append(flat(value))
                taps.append(jnp.concatenate(piece, axis=0))
        lanes = slice(n * outs1, (n + 1) * outs1)
        y = dot(jnp.concatenate(taps, axis=1), w_first[:, lanes])
        for j in range(5):
            base = a1[j + 1 + shift, :, :, lanes]
            value = base.astype(F32) + y[2 * j * cols : 2 * (j + 1) * cols].reshape(base.shape)
            x1[j, 1:3, :, lanes] = value.astype(BF16)
            x1[j, 0, :, lanes] = moved(value[1], 1).astype(BF16)
            x1[j, 3, :, lanes] = moved(value[0], -1).astype(BF16)

    @pl.loop(0, 4)
    def _(k):
        a, b = k // 2, lax.rem(k, 2)
        taps = []
        for p in (0, 1):
            for q in (0, 1):
                piece = []
                for j in range(4):
                    value = x1[j + p, pl.ds(b + q, 2)]
                    factor = jnp.where(a == p, keep[5 + j], 1.0)
                    piece.append(flat(scaled(value, factor)))
                taps.append(jnp.concatenate(piece, axis=0))
        y = dot(jnp.concatenate(taps, axis=1), w_up2[k]).astype(BF16)
        for j in range(4):
            for f in (0, 1):
                at = (2 * j + f) * cols
                a2[2 * j + 1 - a, 2 * f + b] = y[at : at + cols]

    @pl.when(jnp.logical_not(last))
    def _():
        for c in range(chunks):
            attend(c)
        send_parts()

    @pl.loop(0, 8)
    def _(i):
        put(p2, i, act(a2[i].astype(F32), g2))

    mine[5].wait()
    given_w[5].wait_recv()

    @pl.loop(0, 3)
    def _(t):
        taps = []
        for p in range(3):
            for q in range(3):
                piece = []
                for j in range(2):
                    value = p2[2 * t + j + p, q : q + 4]
                    if (p, j) == (0, 0):
                        value = scaled(value, keep[10 + t])
                    elif (p, j) == (2, 1):
                        value = scaled(value, keep[11 + t])
                    piece.append(flat(value))
                taps.append(jnp.concatenate(piece, axis=0))
        y = dot(jnp.concatenate(taps, axis=1), w_second[...])
        for j in range(2):
            base = a2[2 * t + 1 + j]
            put(x2, 2 * t + j,
                base.astype(F32) + y[4 * j * cols : 4 * (j + 1) * cols].reshape(base.shape))

    @pl.when(jnp.logical_not(last))
    def _():
        settle()
        given.start()

    @pl.loop(0, 2)
    def _(a):
        taps = []
        for p in (0, 1):
            for q in range(3):
                piece = []
                for j in range(4):
                    value = x2[j + a + p, q : q + 4]
                    factor = jnp.where(a == p, keep[14 + j + a], 1.0)
                    piece.append(flat(scaled(value, factor)))
                taps.append(jnp.concatenate(piece, axis=0))
        y = dot(jnp.concatenate(taps, axis=1), w_up3[a]).astype(BF16)
        outs3 = a3.shape[-1]
        for j in range(4):
            for f in range(4):
                at = (4 * j + f) * cols
                for b in (0, 1):
                    a3[2 * j + a, 2 * f + b] = y[at : at + cols, b * outs3 : (b + 1) * outs3]

    @pl.loop(0, 8)
    def _(i):
        put(p3, i, act(a3[i].astype(F32), g3))

    @pl.loop(0, 3)
    def _(t):
        taps = []
        for p in range(3):
            for q in range(4):
                piece = []
                for j in range(2):
                    for e in range(4):
                        value = p3[2 * t + j + p, 2 * e + q]
                        if (p, j) == (2, 0) or (p, j) == (0, 1):
                            value = scaled(value, keep[21 + t])
                        piece.append(value)
                taps.append(jnp.concatenate(piece, axis=0))
        y = dot(jnp.concatenate(taps, axis=1), w_third[...])
        outs3 = a3.shape[-1]
        for j in range(2):
            value = jnp.stack([
                y[(4 * j + f // 2) * cols : (4 * j + f // 2 + 1) * cols,
                  (f % 2) * outs3 : (f % 2 + 1) * outs3]
                for f in range(8)
            ])
            value = (a3[2 * t + 1 + j].astype(F32) + value).astype(BF16).astype(F32)
            put(p4, 2 * t + j, act(value, g4))

    p4[0] = scaled(p4[0], keep[21])
    p4[5] = scaled(p4[5], keep[23])
    window = jnp.concatenate(
        [
            jnp.concatenate([p4[s + r, at] for s in range(4)], axis=0)
            for r in range(3)
            for at in range(10)
        ],
        axis=1,
    )
    colors = lax.dot_general(w_color[...], window, NT, preferred_element_type=F32)
    lines = []
    for s in range(4):
        line = []
        for pair in range(4):
            lanes = slice((s // 2) * 128, (s // 2 + 1) * 128)
            even = colors[16 * pair : 16 * pair + 8, lanes]
            odd = colors[16 * pair + 8 : 16 * pair + 16, lanes]
            first = lanes_of(even.shape) < cols
            if s % 2 == 0:
                line.append(jnp.where(first, even, swap_halves(odd)))
            else:
                line.append(jnp.where(first, swap_halves(even), odd))
        lines.append(jnp.concatenate(line, axis=1))
    value = jnp.concatenate(lines, axis=0)
    high = value.astype(BF16)
    rest = value - high.astype(F32)
    middle = rest.astype(BF16)
    final = (rest - middle.astype(F32)).astype(BF16)
    placed = dot(jnp.concatenate([high, middle, final], axis=0), order[...])
    placed = placed[:32] + (placed[32:64] + placed[64:])
    for k in range(picture.shape[0]):
        for s in range(4):
            picture[k, s : s + 1] = placed[8 * s + k : 8 * s + k + 1]

    shown = pltpu.make_async_copy(picture, image.at[section], out_sem)
    shared = pltpu.make_async_remote_copy(
        src_ref=picture, dst_ref=image.at[section], send_sem=send_i, recv_sem=recv_i,
        device_id=partner, device_id_type=MESH,
    )
    shared.start()
    shown.start()

    given.wait_recv()
    given.wait_send()

    @pl.when(last)
    def _():
        side_copy.wait_send()
        for by in (1, -1, 2, -2):
            for t in range(sections):

                @pl.when(inside(by))
                def _():
                    row_copy(by, t, me + by).wait_send()

    @pl.when(jnp.logical_not(last))
    def _():
        sent_all()

    @pl.loop(0, devices)
    def _(d):
        @pl.when(d != me)
        def _():
            part_copy(d, me).wait_send()

    for copy in given_w:
        copy.wait_send()
    shown.wait()
    shared.wait()


def body(
    latents, cond, embed, audio_table, audio_map, out_proj, tile_start,
    conv_input, conv_first, conv_second_up, conv_second, conv_third_up, conv_third, conv_color,
    gain_first, gain_second, gain_third, gain_color,
):
    devices, sections = lax.axis_size("seq"), lax.axis_size("section")
    splits = max(devices // HEADS, 1)
    per = max(HEADS // devices, 1)
    groups = devices // splits
    chunk = 2 if per % 2 == 0 else 1
    chunks = per // chunk
    wide = chunk * HSIZE
    latent = latents[0]
    count, patch = latent.shape
    half = count // splits
    features = cond.shape[-1]
    depth = -(-(patch + audio_table.shape[1]) // 128) * 128
    flat = lambda w: w.reshape(-1, w.shape[-1])
    taps = lambda w: w.reshape(9, *w.shape[2:])
    turned = lambda w: taps(jnp.swapaxes(w, 2, 3))
    c1, c2 = 2 * conv_first.shape[3], 2 * conv_second.shape[3]
    c3 = 2 * conv_third.shape[3]
    rgb = conv_color.shape[3]
    vmem = lambda shape, kind=BF16: pltpu.VMEM(shape, kind)
    dma = pltpu.SemaphoreType.DMA
    hbm = pl.BlockSpec(memory_space=pl.ANY)
    smem = pl.BlockSpec(memory_space=pltpu.SMEM)
    operands = (
        audio_map, tile_start,
        latent, cond[0], embed[0], audio_table[0], out_proj[0].T,
        flat(conv_input), flat(conv_first), taps(conv_second_up), flat(conv_second),
        turned(conv_third_up), turned(conv_third), flat(conv_color).T,
        gain_first[None], gain_second[None], gain_third[None], gain_color[None],
    )
    handed, image = pl.pallas_call(
        functools.partial(step_kernel, splits, per, chunk, sections, devices),
        out_shape=(
            jax.ShapeDtypeStruct(latent.shape, F32),
            jax.ShapeDtypeStruct((2, rgb, 4, 8 * count), F32),
        ),
        in_specs=[smem] * 2 + [hbm] * (len(operands) - 2),
        out_specs=(hbm, hbm),
        scratch_shapes=[
            vmem((count, patch), F32), vmem((count, 2 * patch), F32), vmem((count, depth)),
            vmem((3, count, features)), vmem((depth, features)), vmem((patch, features)),
            vmem((depth, features)), vmem((patch, features)),
            vmem((groups, chunks, count, wide)), vmem((groups, chunks, count, wide + 128)),
            vmem((chunks, devices * half, wide)), vmem((chunks, devices * count, wide + 128)),
            vmem((devices * half, 128), F32),
            vmem((devices, half // 2, 128), F32), vmem((devices, half // 2, 128), F32),
            vmem((count, 2 * patch), F32), vmem((count, patch), F32),
            vmem((count, 2 * patch)), vmem((5, count, 2 * patch)),
            pltpu.SMEM((24,), F32),
            vmem((9 * patch // 4, c1)), vmem((9 * c1, c1)), vmem((9, c1, c2)),
            vmem((9 * c2, c2)), vmem((9, c3, c2)), vmem((9, c3, c3)), vmem((rgb, 9 * c3)),
            vmem((1, c1), F32), vmem((1, c2), F32), vmem((1, c3), F32), vmem((1, c3), F32),
            vmem((4, 4 * patch, c1)), vmem((4, 4 * c1, c2)), vmem((2, 6 * c2, 2 * c3)),
            vmem((12 * c3, 2 * c3)), vmem((64, 30 * c3)), vmem((8 * count, 8 * count)),
            vmem((8, 2, count, c1)), vmem((7, 4, count, c1)), vmem((5, 4, count, c1)),
            vmem((8, 4, count, c2)), vmem((8, 6, count, c2)), vmem((6, 6, count, c2)),
            vmem((8, 8, count, c3)), vmem((8, 10, count, c3)), vmem((6, 10, count, c3)),
            vmem((rgb, 4, 8 * count), F32),
            dma((13,)), dma((chunks, devices)), dma((chunks, devices)),
            dma((chunks, devices)), dma((chunks, devices)), dma((chunks, 2)),
            dma((devices,)), dma((devices,)), dma((6,)), dma((6,)), dma((6,)),
            dma((5, sections)), dma((5,)), dma, dma, dma, dma, dma,
            pltpu.SemaphoreType.REGULAR,
        ],
        compiler_params=pltpu.CompilerParams(
            collective_id=0, has_side_effects=True, vmem_limit_bytes=60 * 1024 * 1024
        ),
    )(*operands)
    image = jnp.swapaxes(image, 0, 1).reshape(rgb, 8, 8 * count)
    return (handed[None], image)


def solution(mesh):
    in_specs = (
        P("section", ("replica", "seq"), None),
        P("section", None, ("replica", "seq"), None),
        P("section", None, None, None),
        P("section", "replica", None),
        P(("replica", "seq")),
        P("section", None, None),
        P("replica"),
        P(None, None, None, "section"),
        P(None, None, None, "section"),
        P(None, None, None, "section"),
        P(None, None, None, "section"),
        P(None, None, None, "section"),
        P(None, None, None, "section"),
        P(),
        P(),
        P(),
        P(),
        P(),
    )
    out_specs = (P("section", ("replica", "seq"), None), P(None, ("replica", "seq"), None))
    return jax.shard_map(body, mesh=mesh, in_specs=in_specs, out_specs=out_specs, check_vma=False)
```

```python
import functools
import math

import jax
import jax.numpy as jnp
from jax import lax
from jax.experimental import pallas as pl
from jax.experimental.pallas import tpu as pltpu
from jax.sharding import PartitionSpec as P

HEADS = 32
HSIZE = 128


step_size = -0.5
norm_eps = 1e-06


MESH = pl.DeviceIdType.MESH
F32, BF16 = jnp.float32, jnp.bfloat16
NT = (((1,), (1,)), ((), ()))


def lanes_of(shape):
    return lax.broadcasted_iota(jnp.int32, shape, len(shape) - 1)


def rows_of(shape):
    return lax.broadcasted_iota(jnp.int32, shape, len(shape) - 2)


def swap_halves(value):
    return pltpu.roll(value, value.shape[1] // 2, 1)


def dot(x, w):
    return jnp.dot(x, w, preferred_element_type=F32)


def scaled(value, factor):
    return value * lax.broadcast(factor, value.shape).astype(BF16)


def pairs(x, y, z):
    return ((x, y + z), (x + y, z))


def lift_second(raw, lifted):
    depth = raw.shape[1]
    chunk = 64

    @pl.loop(0, depth // chunk)
    def _(i):
        row = pl.multiple_of(i * chunk, chunk)
        w = [raw[t, pl.ds(row, chunk)].astype(F32) for t in range(9)]
        by_row = [pairs(w[q], w[3 + q], w[6 + q]) for q in range(3)]
        for a in (0, 1):
            for p in (0, 1):
                cols = pairs(*(by_row[q][a][p] for q in range(3)))
                for b in (0, 1):
                    for q in (0, 1):
                        at = pl.multiple_of((2 * p + q) * depth + row, chunk)
                        lifted[2 * a + b, pl.ds(at, chunk)] = cols[b][q].astype(BF16)


def lift_third_up(raw, lifted):
    outs, depth = raw.shape[1:]
    zero = jnp.zeros((depth, outs), BF16)
    w = [raw[t].astype(F32) for t in range(9)]
    by_row = [pairs(w[q], w[3 + q], w[6 + q]) for q in range(3)]
    for a in (0, 1):
        for p in (0, 1):
            cols = pairs(*(by_row[q][a][p] for q in range(3)))
            for b in (0, 1):
                for at in range(3):
                    inside = 0 <= at - b <= 1
                    block = cols[b][at - b].T.astype(BF16) if inside else zero
                    row = (3 * p + at) * depth
                    lifted[a, row : row + depth, b * outs : (b + 1) * outs] = block


def lift_third(raw, lifted):
    outs, depth = raw.shape[1:]
    zero = jnp.zeros((depth, outs), BF16)
    for r in range(3):
        for at in range(4):
            for e in (0, 1):
                inside = 0 <= at - e <= 2
                block = raw[3 * r + at - e].astype(F32).T.astype(BF16) if inside else zero
                row = (4 * r + at) * depth
                lifted[row : row + depth, e * outs : (e + 1) * outs] = block


def lift_input(raw, lifted, cell):
    chans = cell // 4
    zero = jnp.zeros((chans, raw.shape[1]), BF16)
    for a in (0, 1):
        for b in (0, 1):
            blocks = []
            for p in (0, 1):
                for q in (0, 1):
                    for i in (0, 1):
                        for j in (0, 1):
                            u, v = 2 * p + i - 1 + a, 2 * q + j - 1 + b
                            inside = 0 <= u <= 2 and 0 <= v <= 2
                            row = (3 * u + v) * chans
                            blocks.append(raw[row : row + chans] if inside else zero)
            lifted[2 * a + b] = jnp.concatenate(blocks, axis=0)


def lift_color(raw, lifted):
    color = raw[...].astype(F32)
    color = jnp.concatenate([color, jnp.zeros((8 - color.shape[0], color.shape[1]), F32)], axis=0)
    depth = color.shape[1] // 9
    zero = jnp.zeros((8, depth), F32)
    tile = lambda t: color[:, t * depth : (t + 1) * depth]
    for pair in range(4):
        blocks = []
        for f in (2 * pair, 2 * pair + 1):
            blocks.append(
                jnp.concatenate(
                    [
                        tile(3 * r + at - f) if 0 <= at - f <= 2 else zero
                        for r in range(3)
                        for at in range(10)
                    ],
                    axis=1,
                )
            )
        lifted[16 * pair : 16 * (pair + 1)] = jnp.concatenate(blocks, axis=0).astype(BF16)


def step_kernel(
    splits, per, chunk, sections, devices,
    amap, starts,
    latent, cond, embed, table, out_t,
    c_in, c_first, c_up2, c_second, c_up3, c_third, c_color, gain1, gain2, gain3, gain4,
    handed, image,
    lat, latd, xcat, condv, eq, ek, ev, wt, sq, skv, gq, gkv, acc, part, parts, resd, result,
    low, tokens, keep,
    r_in, w_first, r_up2, w_second, r_up3, r_third, r_color, g1, g2, g3, g4,
    w_in, w_up2, w_up3, w_third, w_color, order,
    a1, p1, x1, a2, p2, x2, a3, p3, p4, picture,
    in_sem, send_q, recv_q, send_kv, recv_kv, own_sem, send_p, recv_p,
    here_sem, send_w, recv_w, send_h, recv_h, send_r, recv_r, send_i, recv_i, out_sem, go,
):
    me = lax.axis_index("seq")
    section = lax.axis_index("section")
    last = section == sections - 1
    partner = {"section": lax.rem(section + 1, sections)}
    groups = devices // splits
    count, patch = lat.shape
    half = count // splits
    wide = chunk * HSIZE
    chunks = per // chunk
    my_group = me // splits
    cols = count

    tokens[...] = jnp.zeros(tokens.shape, BF16)
    barrier = pltpu.get_barrier_semaphore()
    for t in range(sections):
        peer = lax.rem(section + t, sections)

        @pl.loop(0 if t else 1, devices)
        def _(k):
            d = lax.rem(me + k, devices)
            pl.semaphore_signal(
                barrier, inc=1, device_id={"section": peer, "seq": d}, device_id_type=MESH
            )

    frames = table.shape[0]
    loads = [
        pltpu.make_async_copy(src, dst, in_sem.at[k])
        for k, (src, dst) in enumerate(
            (
                (latent, lat), (embed.at[0], eq.at[pl.ds(0, patch)]),
                (table, eq.at[pl.ds(patch, frames)]), (embed.at[2], ev.at[pl.ds(0, patch)]),
                (table, ev.at[pl.ds(patch, frames)]), (embed.at[1], ek), (cond, condv),
                (out_t, wt), (gain1, g1), (gain2, g2), (gain3, g3), (gain4, g4),
                (c_color, r_color),
            )
        )
    ]
    for copy in loads:
        copy.start()

    weights = ((c_third, r_third), (c_in, r_in), (c_up3, r_up3), (c_up2, r_up2),
               (c_first, w_first), (c_second, w_second))

    def half_of(dst, k):
        if k in (0, 2):
            size = dst.shape[1] // 2
            return dst.at[:, pl.ds(pl.multiple_of(section * size, size), size)]
        size = dst.shape[-1] // 2
        lanes = pl.ds(pl.multiple_of(section * size, size), size)
        return dst.at[:, :, lanes] if len(dst.shape) == 3 else dst.at[:, lanes]

    mine = [
        pltpu.make_async_copy(src, half_of(dst, k), here_sem.at[k])
        for k, (src, dst) in enumerate(weights)
    ]
    given_w = [
        pltpu.make_async_remote_copy(
            src_ref=src, dst_ref=half_of(dst, k), send_sem=send_w.at[k], recv_sem=recv_w.at[k],
            device_id=partner, device_id_type=MESH,
        )
        for k, (src, dst) in enumerate(weights)
    ]

    blocks = starts.shape[0]

    def joined(by):
        block = me + by
        inside = jnp.logical_and(block >= 0, block + 1 < blocks)
        begins = starts[jnp.clip(block + 1, 0, blocks - 1)]
        return jnp.where(jnp.logical_and(inside, begins == 0), 1.0, 0.0).astype(F32)

    k_a, k_b, k_c, k_d = (joined(by) for by in (-2, -1, 0, 1))
    one = jnp.float32(1.0)
    upper = section == 0
    either = lambda x, y: jnp.where(upper, x, y)
    level1 = [either(x, y) for x, y in (
        (k_a, one), (one, k_b), (k_b, one), (one, k_c), (k_c, one), (one, k_d))]
    level2 = [either(x, y) for x, y in ((one, k_b), (k_b, one), (one, k_c), (k_c, one))]
    b_or, c_or = either(k_b, one), either(one, k_c)
    for k, value in enumerate(
        [k_a, k_b, k_c, k_d] + level1 + level2 + [one, b_or, one, c_or, one, one, one]
        + [b_or, one, c_or]
    ):
        keep[k] = value

    zrow = patch + frames
    eq[zrow:] = jnp.zeros((eq.shape[0] - zrow, eq.shape[1]), BF16)
    ev[zrow:] = jnp.zeros((ev.shape[0] - zrow, ev.shape[1]), BF16)
    perm_row = rows_of(order.shape)
    perm_col = lanes_of(order.shape)
    phase = lax.div(perm_row, jnp.int32(cols))
    target = (perm_row - phase * cols) * 8 + phase
    order[...] = jnp.where(perm_col == target, 1.0, 0.0).astype(BF16)

    loads[0].wait()
    latd[:, :patch] = lat[...]
    latd[:, patch:] = lat[...]
    row = rows_of(xcat.shape)
    lane = lanes_of(xcat.shape)
    per_block = count // amap.shape[0]
    frame = lax.broadcast(amap[0], xcat.shape)
    for k in range(1, amap.shape[0]):
        frame = jnp.where(row >= k * per_block, amap[k], frame)
    padded = latd[...]
    if xcat.shape[1] > padded.shape[1]:
        extra = xcat.shape[1] - padded.shape[1]
        padded = jnp.concatenate([padded, jnp.zeros((count, extra), F32)], axis=1)
    onehot = jnp.where(lane == frame + patch, 1.0, 0.0)
    xcat[...] = jnp.where(lane < patch, padded, onehot).astype(BF16)
    for copy in loads[1:8]:
        copy.wait()

    def q_copy(c, d, src):
        return pltpu.make_async_remote_copy(
            src_ref=sq.at[d // splits, c, pl.ds(lax.rem(d, splits) * half, half)],
            dst_ref=gq.at[c, pl.ds(src * half, half)],
            send_sem=send_q.at[c, d], recv_sem=recv_q.at[c, src],
            device_id={"seq": d}, device_id_type=MESH,
        )

    def kv_copy(c, d, src):
        return pltpu.make_async_remote_copy(
            src_ref=skv.at[d // splits, c],
            dst_ref=gkv.at[c, pl.ds(src * count, count)],
            send_sem=send_kv.at[c, d], recv_sem=recv_kv.at[c, src],
            device_id={"seq": d}, device_id_type=MESH,
        )

    near = max(groups // 2, 1)
    quarter = max(groups // 4, 1)
    inner = lax.rem((my_group // quarter + 1) // 2, 2)

    def turn(k):
        side = lax.rem(my_group // near + inner + k // near, max(groups // near, 1))
        return side * near + lax.rem(my_group + 1 + lax.rem(k, near), near)

    sharp = math.log2(math.e) / math.sqrt(HSIZE)

    def send(c, g):
        @pl.loop(0, splits)
        def _(r):
            d = g * splits + r

            @pl.when(d != me)
            def _():
                q_copy(c, d, me).start()
                kv_copy(c, d, me).start()

    pl.semaphore_wait(barrier, sections * devices - 1)
    for copy in given_w[:2]:
        copy.start()
    for copy in mine:
        copy.start()

    for c in range(chunks):

        @pl.loop(0, groups)
        def _(k):
            g = turn(k)
            at = pl.ds(pl.multiple_of(g * (per * HSIZE) + c * wide, HSIZE), wide)
            q = dot(xcat[...], eq[:, at]) + condv[0, :, at].astype(F32)
            key = dot(xcat[:, :patch], ek[:, at]) + condv[1, :, at].astype(F32)
            v = dot(xcat[...], ev[:, at]) + condv[2, :, at].astype(F32)
            w = wt[:, at]
            if chunk == 2:
                first = lanes_of(w.shape) < HSIZE
                zero = jnp.zeros(w.shape, BF16)
                w = jnp.concatenate([jnp.where(first, w, zero), jnp.where(first, zero, w)], axis=0)
            else:
                w = jnp.concatenate([w, jnp.zeros((128 - w.shape[0], w.shape[1]), BF16)], axis=0)
            mixed = lax.dot_general(v.astype(BF16), w, NT, preferred_element_type=F32)
            sq[g, c] = q.astype(BF16)
            skv[g, c, :, :wide] = key.astype(BF16)
            skv[g, c, :, wide:] = mixed.astype(BF16)

            @pl.when(last)
            def _():
                send(c, g)

    for copy in given_w[2:]:
        copy.start()

    own = []
    for c in range(chunks):
        own.append(pltpu.make_async_copy(
            sq.at[my_group, c, pl.ds(lax.rem(me, splits) * half, half)],
            gq.at[c, pl.ds(me * half, half)], own_sem.at[c, 0],
        ))
        own.append(pltpu.make_async_copy(
            skv.at[my_group, c], gkv.at[c, pl.ds(me * count, count)], own_sem.at[c, 1]
        ))
    for copy in own:
        copy.start()

    for copy in loads[8:]:
        copy.wait()
    lift_color(r_color, w_color)
    mine[0].wait()
    given_w[0].wait_recv()
    lift_third(r_third, w_third)
    mine[1].wait()
    given_w[1].wait_recv()
    lift_input(r_in, w_in, patch)
    mine[2].wait()
    given_w[2].wait_recv()
    lift_third_up(r_up3, w_up3)
    mine[3].wait()
    given_w[3].wait_recv()
    lift_second(r_up2, w_up2)

    queries = gq.shape[1]
    block = min(256, queries)
    parts_of = queries // block
    lane128 = lanes_of((block, 128))
    both = half // 2

    def attend(c):
        own[2 * c].wait()
        own[2 * c + 1].wait()

        @pl.loop(0, devices)
        def _(d):
            @pl.when(d != me)
            def _():
                q_copy(c, d, d).wait_recv()
                kv_copy(c, d, d).wait_recv()

        @pl.loop(0, parts_of)
        def _(i):
            at = pl.ds(pl.multiple_of(i * block, block), block)
            outs = []
            for h in range(chunk):
                own_lanes = slice(h * HSIZE, (h + 1) * HSIZE)
                scores = lax.dot_general(
                    gq[c, at, own_lanes], gkv[c, :, own_lanes], NT, preferred_element_type=F32
                ) * sharp
                top = jnp.max(scores, axis=1, keepdims=True)
                values = gkv[c, :, wide:]
                values = jnp.concatenate([values, jnp.ones(values.shape, BF16)], axis=1)
                summed = dot(jnp.exp2(scores - top).astype(BF16), values)
                outs.append(summed[:, :128] / summed[:, 128:])
            value = outs[0] if chunk == 1 else jnp.where(lane128 < patch, outs[0], outs[1])
            if c > 0:
                value = value + acc[at]
            if c < chunks - 1:
                acc[at] = value
            else:
                value = value + swap_halves(value)
                for k in range(block // half):
                    low_rows = value[k * half : k * half + both]
                    high_rows = value[k * half + both : (k + 1) * half]
                    first = lanes_of(low_rows.shape) < patch
                    part[i * (block // half) + k] = jnp.where(first, low_rows, high_rows)

    def part_copy(d, src):
        return pltpu.make_async_remote_copy(
            src_ref=part.at[d], dst_ref=parts.at[src],
            send_sem=send_p.at[d], recv_sem=recv_p.at[src],
            device_id={"seq": d}, device_id_type=MESH,
        )

    def send_parts():
        @pl.loop(1, devices)
        def _(k):
            part_copy(lax.rem(me + k, devices), me).start()

    def settle():
        @pl.loop(0, devices)
        def _(d):
            @pl.when(d != me)
            def _():
                part_copy(d, d).wait_recv()

        for r in range(splits):
            total = jnp.zeros((both, 128), F32)
            for g in range(groups):
                d = g * splits + r
                total = total + jnp.where(d == me, part[d], parts[d])
            first = lanes_of(total.shape) < patch
            other = swap_halves(total)
            at = r * half
            low_rows = jnp.where(first, total, other)
            high_rows = jnp.where(first, other, total)
            resd[at : at + both] = latd[at : at + both] + step_size * low_rows
            resd[at + both : at + half] = latd[at + both : at + half] + step_size * high_rows
        result[...] = resd[:, :patch]

    given = pltpu.make_async_remote_copy(
        src_ref=result, dst_ref=handed, send_sem=send_r, recv_sem=recv_r,
        device_id=partner, device_id_type=MESH,
    )

    def row_copy(by, t, to):
        return pltpu.make_async_remote_copy(
            src_ref=low, dst_ref=tokens.at[2 - by],
            send_sem=send_h.at[2 - by, t], recv_sem=recv_h.at[2 - by],
            device_id={"section": t, "seq": lax.rem(to + devices, devices)}, device_id_type=MESH,
        )

    side_copy = pltpu.make_async_remote_copy(
        src_ref=low, dst_ref=tokens.at[2], send_sem=send_h.at[2, 0], recv_sem=recv_h.at[2],
        device_id=partner, device_id_type=MESH,
    )

    def inside(by):
        return jnp.logical_and(me + by >= 0, me + by < devices)

    def sent_all():
        @pl.loop(0, devices)
        def _(d):
            @pl.when(d != me)
            def _():
                for c in range(chunks):
                    q_copy(c, d, me).wait_send()
                    kv_copy(c, d, me).wait_send()

    @pl.when(last)
    def _():
        for c in range(chunks):
            if c == chunks - 1:
                sent_all()
                pl.semaphore_signal(go, inc=1, device_id=partner, device_id_type=MESH)
            attend(c)
        send_parts()
        settle()
        low[...] = resd[...].astype(BF16)
        for by in (1, -1, 2, -2):
            for t in range(sections):

                @pl.when(inside(by))
                def _():
                    row_copy(by, t, me + by).start()

        side_copy.start()
        given.start()
        tokens[2] = low[...]

    @pl.when(jnp.logical_not(last))
    def _():
        pl.semaphore_wait(go, 1)
        for c in range(chunks):

            @pl.loop(0, groups)
            def _(k):
                send(c, turn(k))

        side_copy.wait_recv()

    for by in (1, -1, 2, -2):

        @pl.when(inside(-by))
        def _():
            row_copy(by, 0, me - by).wait_recv()

    def moved(value, by):
        position = rows_of(value.shape)
        if by > 0:
            return jnp.where(position > 0, pltpu.roll(value, 1, 0), 0.0)
        return jnp.where(position < cols - 1, pltpu.roll(value, cols - 1, 0), 0.0)

    def put(buf, index, value):
        phases = value.shape[0]
        buf[index, 1 : phases + 1] = value.astype(BF16)
        buf[index, 0] = moved(value[phases - 1], 1).astype(BF16)
        buf[index, phases + 1] = moved(value[0], -1).astype(BF16)

    def act(value, gain):
        square = jnp.mean(value * value, axis=-1, keepdims=True)
        h = value * (0.5 * lax.rsqrt(square + norm_eps)) * gain[...]
        return h + h * jnp.tanh(h)

    def flat(value):
        return value.reshape(-1, value.shape[-1])

    cells = []
    for i in range(5):
        value = tokens[i].astype(F32)
        first = lanes_of(value.shape) < patch
        cells.append((
            jnp.where(first, moved(value, 1), value).astype(BF16),
            jnp.where(first, value, moved(value, -1)).astype(BF16),
        ))
    for a in (0, 1):
        for b in (0, 1):
            x = []
            for j in range(4):
                above, below = cells[j][b], cells[j + 1][b]
                if a == 0:
                    above = scaled(above, keep[j])
                else:
                    below = scaled(below, keep[j])
                x.append(jnp.concatenate([above, below], axis=1))
            y = dot(jnp.concatenate(x, axis=0), w_in[2 * a + b]).astype(BF16)
            for j in range(4):
                a1[2 * j + 1 - a, b] = y[j * cols : (j + 1) * cols]

    shift = section

    for i in range(7):
        put(p1, i, act(a1[i + shift].astype(F32), g1))

    mine[4].wait()
    given_w[4].wait_recv()
    outs1 = w_first.shape[1] // 2
    for n in range(2):
        taps = []
        for p in range(3):
            for q in range(3):
                piece = []
                for j in range(5):
                    value = p1[j + p, q : q + 2]
                    if p == 0:
                        value = scaled(value, keep[4 + j])
                    elif p == 2:
                        value = scaled(value, keep[5 + j])
                    piece.append(flat(value))
                taps.append(jnp.concatenate(piece, axis=0))
        lanes = slice(n * outs1, (n + 1) * outs1)
        y = dot(jnp.concatenate(taps, axis=1), w_first[:, lanes])
        for j in range(5):
            base = a1[j + 1 + shift, :, :, lanes]
            value = base.astype(F32) + y[2 * j * cols : 2 * (j + 1) * cols].reshape(base.shape)
            x1[j, 1:3, :, lanes] = value.astype(BF16)
            x1[j, 0, :, lanes] = moved(value[1], 1).astype(BF16)
            x1[j, 3, :, lanes] = moved(value[0], -1).astype(BF16)

    for k in range(4):
        a, b = k // 2, k % 2
        taps = []
        for p in (0, 1):
            for q in (0, 1):
                piece = []
                for j in range(4):
                    value = x1[j + p, b + q : b + q + 2]
                    piece.append(flat(scaled(value, keep[5 + j]) if a == p else value))
                taps.append(jnp.concatenate(piece, axis=0))
        y = dot(jnp.concatenate(taps, axis=1), w_up2[k]).astype(BF16)
        for j in range(4):
            for f in (0, 1):
                at = (2 * j + f) * cols
                a2[2 * j + 1 - a, 2 * f + b] = y[at : at + cols]

    for i in range(8):
        put(p2, i, act(a2[i].astype(F32), g2))

    mine[5].wait()
    given_w[5].wait_recv()

    for t in range(3):
        taps = []
        for p in range(3):
            for q in range(3):
                piece = []
                for j in range(2):
                    value = p2[2 * t + j + p, q : q + 4]
                    if (p, j) == (0, 0):
                        value = scaled(value, keep[10 + t])
                    elif (p, j) == (2, 1):
                        value = scaled(value, keep[11 + t])
                    piece.append(flat(value))
                taps.append(jnp.concatenate(piece, axis=0))
        y = dot(jnp.concatenate(taps, axis=1), w_second[...])
        for j in range(2):
            base = a2[2 * t + 1 + j]
            put(x2, 2 * t + j,
                base.astype(F32) + y[4 * j * cols : 4 * (j + 1) * cols].reshape(base.shape))

    @pl.when(jnp.logical_not(last))
    def _():
        for c in range(chunks):
            attend(c)
        send_parts()

    for a in range(2):
        taps = []
        for p in (0, 1):
            for q in range(3):
                piece = []
                for j in range(4):
                    value = x2[j + a + p, q : q + 4]
                    if a == p and j + a in (1, 3):
                        value = scaled(value, keep[14 + j + a])
                    piece.append(flat(value))
                taps.append(jnp.concatenate(piece, axis=0))
        y = dot(jnp.concatenate(taps, axis=1), w_up3[a]).astype(BF16)
        outs3 = a3.shape[-1]
        for j in range(4):
            for f in range(4):
                at = (4 * j + f) * cols
                for b in (0, 1):
                    a3[2 * j + a, 2 * f + b] = y[at : at + cols, b * outs3 : (b + 1) * outs3]

    for i in range(8):
        put(p3, i, act(a3[i].astype(F32), g3))

    @pl.when(jnp.logical_not(last))
    def _():
        settle()
        given.start()

    for t in range(3):
        taps = []
        for p in range(3):
            for q in range(4):
                piece = []
                for j in range(2):
                    for e in range(4):
                        value = p3[2 * t + j + p, 2 * e + q]
                        if t != 1 and (p, j) in ((2, 0), (0, 1)):
                            value = scaled(value, keep[21 + t])
                        piece.append(value)
                taps.append(jnp.concatenate(piece, axis=0))
        y = dot(jnp.concatenate(taps, axis=1), w_third[...])
        outs3 = a3.shape[-1]
        for j in range(2):
            value = jnp.stack([
                y[(4 * j + f // 2) * cols : (4 * j + f // 2 + 1) * cols,
                  (f % 2) * outs3 : (f % 2 + 1) * outs3]
                for f in range(8)
            ])
            value = (a3[2 * t + 1 + j].astype(F32) + value).astype(BF16).astype(F32)
            put(p4, 2 * t + j, act(value, g4))

    p4[0] = scaled(p4[0], keep[21])
    p4[5] = scaled(p4[5], keep[23])
    window = jnp.concatenate(
        [
            jnp.concatenate([p4[s + r, at] for s in range(4)], axis=0)
            for r in range(3)
            for at in range(10)
        ],
        axis=1,
    )
    colors = lax.dot_general(w_color[...], window, NT, preferred_element_type=F32)
    lines = []
    for s in range(4):
        line = []
        for pair in range(4):
            lanes = slice((s // 2) * 128, (s // 2 + 1) * 128)
            even = colors[16 * pair : 16 * pair + 8, lanes]
            odd = colors[16 * pair + 8 : 16 * pair + 16, lanes]
            first = lanes_of(even.shape) < cols
            if s % 2 == 0:
                line.append(jnp.where(first, even, swap_halves(odd)))
            else:
                line.append(jnp.where(first, swap_halves(even), odd))
        lines.append(jnp.concatenate(line, axis=1))
    value = jnp.concatenate(lines, axis=0)
    high = value.astype(BF16)
    rest = value - high.astype(F32)
    middle = rest.astype(BF16)
    final = (rest - middle.astype(F32)).astype(BF16)
    placed = dot(jnp.concatenate([high, middle, final], axis=0), order[...])
    placed = placed[:32] + (placed[32:64] + placed[64:])
    for k in range(picture.shape[0]):
        for s in range(4):
            picture[k, s : s + 1] = placed[8 * s + k : 8 * s + k + 1]

    shown = pltpu.make_async_copy(picture, image.at[section], out_sem)
    shared = pltpu.make_async_remote_copy(
        src_ref=picture, dst_ref=image.at[section], send_sem=send_i, recv_sem=recv_i,
        device_id=partner, device_id_type=MESH,
    )
    shared.start()
    shown.start()

    given.wait_recv()
    given.wait_send()

    @pl.when(last)
    def _():
        side_copy.wait_send()
        for by in (1, -1, 2, -2):
            for t in range(sections):

                @pl.when(inside(by))
                def _():
                    row_copy(by, t, me + by).wait_send()

    @pl.when(jnp.logical_not(last))
    def _():
        sent_all()

    @pl.loop(0, devices)
    def _(d):
        @pl.when(d != me)
        def _():
            part_copy(d, me).wait_send()

    for copy in given_w:
        copy.wait_send()
    shown.wait()
    shared.wait()


def finish_kernel(handed, image, handed_out, image_out):
    handed_out[...] = handed[...]
    for s in range(2):
        image_out[:, 4 * s : 4 * s + 4] = image[s]


def body(
    latents, cond, embed, audio_table, audio_map, out_proj, tile_start,
    conv_input, conv_first, conv_second_up, conv_second, conv_third_up, conv_third, conv_color,
    gain_first, gain_second, gain_third, gain_color,
):
    devices, sections = lax.axis_size("seq"), lax.axis_size("section")
    splits = max(devices // HEADS, 1)
    per = max(HEADS // devices, 1)
    groups = devices // splits
    chunk = 2 if per % 2 == 0 else 1
    chunks = per // chunk
    wide = chunk * HSIZE
    latent = latents[0]
    count, patch = latent.shape
    half = count // splits
    features = cond.shape[-1]
    depth = -(-(patch + audio_table.shape[1]) // 128) * 128
    flat = lambda w: w.reshape(-1, w.shape[-1])
    taps = lambda w: w.reshape(9, *w.shape[2:])
    turned = lambda w: taps(jnp.swapaxes(w, 2, 3))
    c1, c2 = 2 * conv_first.shape[3], 2 * conv_second.shape[3]
    c3 = 2 * conv_third.shape[3]
    rgb = conv_color.shape[3]
    vmem = lambda shape, kind=BF16: pltpu.VMEM(shape, kind)
    dma = pltpu.SemaphoreType.DMA
    hbm = pl.BlockSpec(memory_space=pl.ANY)
    smem = pl.BlockSpec(memory_space=pltpu.SMEM)
    whole = pl.BlockSpec(memory_space=pltpu.VMEM)
    operands = (
        audio_map, tile_start,
        latent, cond[0], embed[0], audio_table[0], out_proj[0].T,
        flat(conv_input), flat(conv_first), taps(conv_second_up), flat(conv_second),
        turned(conv_third_up), turned(conv_third), flat(conv_color).T,
        gain_first[None], gain_second[None], gain_third[None], gain_color[None],
    )
    handed, image = pl.pallas_call(
        functools.partial(step_kernel, splits, per, chunk, sections, devices),
        out_shape=(
            jax.ShapeDtypeStruct(latent.shape, F32),
            jax.ShapeDtypeStruct((2, rgb, 4, 8 * count), F32),
        ),
        in_specs=[smem] * 2 + [hbm] * (len(operands) - 2),
        out_specs=(whole, whole),
        scratch_shapes=[
            vmem((count, patch), F32), vmem((count, 2 * patch), F32), vmem((count, depth)),
            vmem((3, count, features)), vmem((depth, features)), vmem((patch, features)),
            vmem((depth, features)), vmem((patch, features)),
            vmem((groups, chunks, count, wide)), vmem((groups, chunks, count, wide + 128)),
            vmem((chunks, devices * half, wide)), vmem((chunks, devices * count, wide + 128)),
            vmem((devices * half, 128), F32),
            vmem((devices, half // 2, 128), F32), vmem((devices, half // 2, 128), F32),
            vmem((count, 2 * patch), F32), vmem((count, patch), F32),
            vmem((count, 2 * patch)), vmem((5, count, 2 * patch)),
            pltpu.SMEM((24,), F32),
            vmem((9 * patch // 4, c1)), vmem((9 * c1, c1)), vmem((9, c1, c2)),
            vmem((9 * c2, c2)), vmem((9, c3, c2)), vmem((9, c3, c3)), vmem((rgb, 9 * c3)),
            vmem((1, c1), F32), vmem((1, c2), F32), vmem((1, c3), F32), vmem((1, c3), F32),
            vmem((4, 4 * patch, c1)), vmem((4, 4 * c1, c2)), vmem((2, 6 * c2, 2 * c3)),
            vmem((12 * c3, 2 * c3)), vmem((64, 30 * c3)), vmem((8 * count, 8 * count)),
            vmem((8, 2, count, c1)), vmem((7, 4, count, c1)), vmem((5, 4, count, c1)),
            vmem((8, 4, count, c2)), vmem((8, 6, count, c2)), vmem((6, 6, count, c2)),
            vmem((8, 8, count, c3)), vmem((8, 10, count, c3)), vmem((6, 10, count, c3)),
            vmem((rgb, 4, 8 * count), F32),
            dma((13,)), dma((chunks, devices)), dma((chunks, devices)),
            dma((chunks, devices)), dma((chunks, devices)), dma((chunks, 2)),
            dma((devices,)), dma((devices,)), dma((6,)), dma((6,)), dma((6,)),
            dma((5, sections)), dma((5,)), dma, dma, dma, dma, dma,
            pltpu.SemaphoreType.REGULAR,
        ],
        compiler_params=pltpu.CompilerParams(
            collective_id=0, has_side_effects=True, vmem_limit_bytes=60 * 1024 * 1024
        ),
    )(*operands)
    handed, image = pl.pallas_call(
        finish_kernel,
        out_shape=(
            jax.ShapeDtypeStruct(latent.shape, F32),
            jax.ShapeDtypeStruct((rgb, 8, 8 * count), F32),
        ),
        in_specs=[whole, whole],
        out_specs=(whole, whole),
    )(handed, image)
    return (handed[None], image)


def solution(mesh):
    in_specs = (
        P("section", ("replica", "seq"), None),
        P("section", None, ("replica", "seq"), None),
        P("section", None, None, None),
        P("section", "replica", None),
        P(("replica", "seq")),
        P("section", None, None),
        P("replica"),
        P(None, None, None, "section"),
        P(None, None, None, "section"),
        P(None, None, None, "section"),
        P(None, None, None, "section"),
        P(None, None, None, "section"),
        P(None, None, None, "section"),
        P(),
        P(),
        P(),
        P(),
        P(),
    )
    out_specs = (P("section", ("replica", "seq"), None), P(None, ("replica", "seq"), None))
    return jax.shard_map(body, mesh=mesh, in_specs=in_specs, out_specs=out_specs, check_vma=False)
```

```python
import functools
import math

import jax
import jax.numpy as jnp
from jax import lax
from jax.experimental import pallas as pl
from jax.experimental.pallas import tpu as pltpu
from jax.sharding import PartitionSpec as P

HEADS = 32
HSIZE = 128


step_size = -0.5
norm_eps = 1e-06


MESH = pl.DeviceIdType.MESH
F32, BF16 = jnp.float32, jnp.bfloat16
NT = (((1,), (1,)), ((), ()))


def lanes_of(shape):
    return lax.broadcasted_iota(jnp.int32, shape, len(shape) - 1)


def rows_of(shape):
    return lax.broadcasted_iota(jnp.int32, shape, len(shape) - 2)


def swap_halves(value):
    return pltpu.roll(value, value.shape[1] // 2, 1)


def dot(x, w):
    return jnp.dot(x, w, preferred_element_type=F32)


def scaled(value, factor):
    return value * lax.broadcast(factor, value.shape).astype(BF16)


def pairs(x, y, z):
    return ((x, y + z), (x + y, z))


def lift_second(raw, lifted):
    depth = raw.shape[1]
    chunk = 64

    @pl.loop(0, depth // chunk)
    def _(i):
        row = pl.multiple_of(i * chunk, chunk)
        w = [raw[t, pl.ds(row, chunk)].astype(F32) for t in range(9)]
        by_row = [pairs(w[q], w[3 + q], w[6 + q]) for q in range(3)]
        for a in (0, 1):
            for p in (0, 1):
                cols = pairs(*(by_row[q][a][p] for q in range(3)))
                for b in (0, 1):
                    for q in (0, 1):
                        at = pl.multiple_of((2 * p + q) * depth + row, chunk)
                        lifted[2 * a + b, pl.ds(at, chunk)] = cols[b][q].astype(BF16)


def lift_third_up(raw, lifted):
    outs, depth = raw.shape[1:]
    zero = jnp.zeros((depth, outs), BF16)
    w = [raw[t].astype(F32) for t in range(9)]
    by_row = [pairs(w[q], w[3 + q], w[6 + q]) for q in range(3)]
    for a in (0, 1):
        for p in (0, 1):
            cols = pairs(*(by_row[q][a][p] for q in range(3)))
            for b in (0, 1):
                for at in range(3):
                    inside = 0 <= at - b <= 1
                    block = cols[b][at - b].T.astype(BF16) if inside else zero
                    row = (3 * p + at) * depth
                    lifted[a, row : row + depth, b * outs : (b + 1) * outs] = block


def lift_third(raw, lifted):
    outs, depth = raw.shape[1:]
    zero = jnp.zeros((depth, outs), BF16)
    for r in range(3):
        for at in range(4):
            for e in (0, 1):
                inside = 0 <= at - e <= 2
                block = raw[3 * r + at - e].astype(F32).T.astype(BF16) if inside else zero
                row = (4 * r + at) * depth
                lifted[row : row + depth, e * outs : (e + 1) * outs] = block


def lift_input(raw, lifted, cell):
    chans = cell // 4
    zero = jnp.zeros((chans, raw.shape[1]), BF16)
    for a in (0, 1):
        for b in (0, 1):
            blocks = []
            for p in (0, 1):
                for q in (0, 1):
                    for i in (0, 1):
                        for j in (0, 1):
                            u, v = 2 * p + i - 1 + a, 2 * q + j - 1 + b
                            inside = 0 <= u <= 2 and 0 <= v <= 2
                            row = (3 * u + v) * chans
                            blocks.append(raw[row : row + chans] if inside else zero)
            lifted[2 * a + b] = jnp.concatenate(blocks, axis=0)


def lift_color(raw, lifted):
    color = raw[...].astype(F32)
    color = jnp.concatenate([color, jnp.zeros((8 - color.shape[0], color.shape[1]), F32)], axis=0)
    depth = color.shape[1] // 9
    zero = jnp.zeros((8, depth), F32)
    tile = lambda t: color[:, t * depth : (t + 1) * depth]
    for pair in range(4):
        blocks = []
        for f in (2 * pair, 2 * pair + 1):
            blocks.append(
                jnp.concatenate(
                    [
                        tile(3 * r + at - f) if 0 <= at - f <= 2 else zero
                        for r in range(3)
                        for at in range(10)
                    ],
                    axis=1,
                )
            )
        lifted[16 * pair : 16 * (pair + 1)] = jnp.concatenate(blocks, axis=0).astype(BF16)


def step_kernel(
    splits, per, chunk, sections, devices,
    amap, starts,
    latent, cond, embed, table, out_t,
    c_in, c_first, c_up2, c_second, c_up3, c_third, c_color, gain1, gain2, gain3, gain4,
    handed, image,
    lat, latd, xcat, condv, eq, ek, ev, wt, sq, skv, gq, gkv, acc, part, parts, resd, result,
    low, tokens, keep,
    r_in, w_first, r_up2, w_second, r_up3, r_third, r_color, g1, g2, g3, g4,
    w_in, w_up2, w_up3, w_third, w_color, order,
    a1, p1, x1, a2, p2, x2, a3, p3, p4, picture,
    in_sem, send_q, recv_q, send_kv, recv_kv, own_sem, send_p, recv_p,
    here_sem, send_w, recv_w, send_h, recv_h, send_r, recv_r, send_i, recv_i, out_sem, go,
):
    me = lax.axis_index("seq")
    section = lax.axis_index("section")
    last = section == sections - 1
    partner = {"section": lax.rem(section + 1, sections)}
    groups = devices // splits
    count, patch = lat.shape
    half = count // splits
    wide = chunk * HSIZE
    chunks = per // chunk
    my_group = me // splits
    cols = count

    tokens[...] = jnp.zeros(tokens.shape, BF16)
    barrier = pltpu.get_barrier_semaphore()
    for t in range(sections):
        peer = lax.rem(section + t, sections)

        @pl.loop(0 if t else 1, devices)
        def _(k):
            d = lax.rem(me + k, devices)
            pl.semaphore_signal(
                barrier, inc=1, device_id={"section": peer, "seq": d}, device_id_type=MESH
            )

    frames = table.shape[0]
    loads = [
        pltpu.make_async_copy(src, dst, in_sem.at[k])
        for k, (src, dst) in enumerate(
            (
                (latent, lat), (embed.at[0], eq.at[pl.ds(0, patch)]),
                (table, eq.at[pl.ds(patch, frames)]), (embed.at[2], ev.at[pl.ds(0, patch)]),
                (table, ev.at[pl.ds(patch, frames)]), (embed.at[1], ek), (cond, condv),
                (out_t, wt), (gain1, g1), (gain2, g2), (gain3, g3), (gain4, g4),
                (c_color, r_color),
            )
        )
    ]
    for copy in loads:
        copy.start()

    weights = ((c_third, r_third), (c_in, r_in), (c_up3, r_up3), (c_up2, r_up2),
               (c_first, w_first), (c_second, w_second))

    def half_of(dst, k):
        if k in (0, 2):
            size = dst.shape[1] // 2
            return dst.at[:, pl.ds(pl.multiple_of(section * size, size), size)]
        size = dst.shape[-1] // 2
        lanes = pl.ds(pl.multiple_of(section * size, size), size)
        return dst.at[:, :, lanes] if len(dst.shape) == 3 else dst.at[:, lanes]

    mine = [
        pltpu.make_async_copy(src, half_of(dst, k), here_sem.at[k])
        for k, (src, dst) in enumerate(weights)
    ]
    given_w = [
        pltpu.make_async_remote_copy(
            src_ref=src, dst_ref=half_of(dst, k), send_sem=send_w.at[k], recv_sem=recv_w.at[k],
            device_id=partner, device_id_type=MESH,
        )
        for k, (src, dst) in enumerate(weights)
    ]

    blocks = starts.shape[0]

    def joined(by):
        block = me + by
        inside = jnp.logical_and(block >= 0, block + 1 < blocks)
        begins = starts[jnp.clip(block + 1, 0, blocks - 1)]
        return jnp.where(jnp.logical_and(inside, begins == 0), 1.0, 0.0).astype(F32)

    k_a, k_b, k_c, k_d = (joined(by) for by in (-2, -1, 0, 1))
    one = jnp.float32(1.0)
    upper = section == 0
    either = lambda x, y: jnp.where(upper, x, y)
    level1 = [either(x, y) for x, y in (
        (k_a, one), (one, k_b), (k_b, one), (one, k_c), (k_c, one), (one, k_d))]
    level2 = [either(x, y) for x, y in ((one, k_b), (k_b, one), (one, k_c), (k_c, one))]
    b_or, c_or = either(k_b, one), either(one, k_c)
    for k, value in enumerate(
        [k_a, k_b, k_c, k_d] + level1 + level2 + [one, b_or, one, c_or, one, one, one]
        + [b_or, one, c_or]
    ):
        keep[k] = value

    zrow = patch + frames
    eq[zrow:] = jnp.zeros((eq.shape[0] - zrow, eq.shape[1]), BF16)
    ev[zrow:] = jnp.zeros((ev.shape[0] - zrow, ev.shape[1]), BF16)
    perm_row = rows_of(order.shape)
    perm_col = lanes_of(order.shape)
    phase = lax.div(perm_row, jnp.int32(cols))
    target = (perm_row - phase * cols) * 8 + phase
    order[...] = jnp.where(perm_col == target, 1.0, 0.0).astype(BF16)

    loads[0].wait()
    latd[:, :patch] = lat[...]
    latd[:, patch:] = lat[...]
    row = rows_of(xcat.shape)
    lane = lanes_of(xcat.shape)
    per_block = count // amap.shape[0]
    frame = lax.broadcast(amap[0], xcat.shape)
    for k in range(1, amap.shape[0]):
        frame = jnp.where(row >= k * per_block, amap[k], frame)
    padded = latd[...]
    if xcat.shape[1] > padded.shape[1]:
        extra = xcat.shape[1] - padded.shape[1]
        padded = jnp.concatenate([padded, jnp.zeros((count, extra), F32)], axis=1)
    onehot = jnp.where(lane == frame + patch, 1.0, 0.0)
    xcat[...] = jnp.where(lane < patch, padded, onehot).astype(BF16)
    for copy in loads[1:8]:
        copy.wait()

    def q_copy(c, d, src):
        return pltpu.make_async_remote_copy(
            src_ref=sq.at[d // splits, c, pl.ds(lax.rem(d, splits) * half, half)],
            dst_ref=gq.at[c, pl.ds(src * half, half)],
            send_sem=send_q.at[c, d], recv_sem=recv_q.at[c, src],
            device_id={"seq": d}, device_id_type=MESH,
        )

    def kv_copy(c, d, src):
        return pltpu.make_async_remote_copy(
            src_ref=skv.at[d // splits, c],
            dst_ref=gkv.at[c, pl.ds(src * count, count)],
            send_sem=send_kv.at[c, d], recv_sem=recv_kv.at[c, src],
            device_id={"seq": d}, device_id_type=MESH,
        )

    near = max(groups // 2, 1)
    quarter = max(groups // 4, 1)
    inner = lax.rem((my_group // quarter + 1) // 2, 2)

    def turn(k):
        side = lax.rem(my_group // near + inner + k // near, max(groups // near, 1))
        return side * near + lax.rem(my_group + 1 + lax.rem(k, near), near)

    sharp = math.log2(math.e) / math.sqrt(HSIZE)

    def send(c, g):
        @pl.loop(0, splits)
        def _(r):
            d = g * splits + r

            @pl.when(d != me)
            def _():
                q_copy(c, d, me).start()
                kv_copy(c, d, me).start()

    pl.semaphore_wait(barrier, sections * devices - 1)
    for copy in given_w[:2]:
        copy.start()
    for copy in mine:
        copy.start()

    for c in range(chunks):

        @pl.loop(0, groups)
        def _(k):
            g = turn(k)
            at = pl.ds(pl.multiple_of(g * (per * HSIZE) + c * wide, HSIZE), wide)
            q = dot(xcat[...], eq[:, at]) + condv[0, :, at].astype(F32)
            key = dot(xcat[:, :patch], ek[:, at]) + condv[1, :, at].astype(F32)
            v = dot(xcat[...], ev[:, at]) + condv[2, :, at].astype(F32)
            w = wt[:, at]
            if chunk == 2:
                first = lanes_of(w.shape) < HSIZE
                zero = jnp.zeros(w.shape, BF16)
                w = jnp.concatenate([jnp.where(first, w, zero), jnp.where(first, zero, w)], axis=0)
            else:
                w = jnp.concatenate([w, jnp.zeros((128 - w.shape[0], w.shape[1]), BF16)], axis=0)
            mixed = lax.dot_general(v.astype(BF16), w, NT, preferred_element_type=F32)
            sq[g, c] = q.astype(BF16)
            skv[g, c, :, :wide] = key.astype(BF16)
            skv[g, c, :, wide:] = mixed.astype(BF16)

            @pl.when(last)
            def _():
                send(c, g)

    for copy in given_w[2:]:
        copy.start()

    own = []
    for c in range(chunks):
        own.append(pltpu.make_async_copy(
            sq.at[my_group, c, pl.ds(lax.rem(me, splits) * half, half)],
            gq.at[c, pl.ds(me * half, half)], own_sem.at[c, 0],
        ))
        own.append(pltpu.make_async_copy(
            skv.at[my_group, c], gkv.at[c, pl.ds(me * count, count)], own_sem.at[c, 1]
        ))
    for copy in own:
        copy.start()

    for copy in loads[8:]:
        copy.wait()
    lift_color(r_color, w_color)
    mine[0].wait()
    given_w[0].wait_recv()
    lift_third(r_third, w_third)
    mine[1].wait()
    given_w[1].wait_recv()
    lift_input(r_in, w_in, patch)
    mine[2].wait()
    given_w[2].wait_recv()
    lift_third_up(r_up3, w_up3)
    mine[3].wait()
    given_w[3].wait_recv()
    lift_second(r_up2, w_up2)

    queries = gq.shape[1]
    block = min(256, queries)
    parts_of = queries // block
    lane128 = lanes_of((block, 128))
    both = half // 2

    def attend(c):
        own[2 * c].wait()
        own[2 * c + 1].wait()

        @pl.loop(0, devices)
        def _(d):
            @pl.when(d != me)
            def _():
                q_copy(c, d, d).wait_recv()
                kv_copy(c, d, d).wait_recv()

        @pl.loop(0, parts_of)
        def _(i):
            at = pl.ds(pl.multiple_of(i * block, block), block)
            outs = []
            for h in range(chunk):
                own_lanes = slice(h * HSIZE, (h + 1) * HSIZE)
                scores = lax.dot_general(
                    gq[c, at, own_lanes], gkv[c, :, own_lanes], NT, preferred_element_type=F32
                ) * sharp
                top = jnp.max(scores, axis=1, keepdims=True)
                values = gkv[c, :, wide:]
                values = jnp.concatenate([values, jnp.ones(values.shape, BF16)], axis=1)
                summed = dot(jnp.exp2(scores - top).astype(BF16), values)
                outs.append(summed[:, :128] / summed[:, 128:])
            value = outs[0] if chunk == 1 else jnp.where(lane128 < patch, outs[0], outs[1])
            if c > 0:
                value = value + acc[at]
            if c < chunks - 1:
                acc[at] = value
            else:
                value = value + swap_halves(value)
                for k in range(block // half):
                    low_rows = value[k * half : k * half + both]
                    high_rows = value[k * half + both : (k + 1) * half]
                    first = lanes_of(low_rows.shape) < patch
                    part[i * (block // half) + k] = jnp.where(first, low_rows, high_rows)

    def part_copy(d, src):
        return pltpu.make_async_remote_copy(
            src_ref=part.at[d], dst_ref=parts.at[src],
            send_sem=send_p.at[d], recv_sem=recv_p.at[src],
            device_id={"seq": d}, device_id_type=MESH,
        )

    def send_parts():
        @pl.loop(1, devices)
        def _(k):
            part_copy(lax.rem(me + k, devices), me).start()

    def settle():
        @pl.loop(0, devices)
        def _(d):
            @pl.when(d != me)
            def _():
                part_copy(d, d).wait_recv()

        for r in range(splits):
            total = jnp.zeros((both, 128), F32)
            for g in range(groups):
                d = g * splits + r
                total = total + jnp.where(d == me, part[d], parts[d])
            first = lanes_of(total.shape) < patch
            other = swap_halves(total)
            at = r * half
            low_rows = jnp.where(first, total, other)
            high_rows = jnp.where(first, other, total)
            resd[at : at + both] = latd[at : at + both] + step_size * low_rows
            resd[at + both : at + half] = latd[at + both : at + half] + step_size * high_rows
        result[...] = resd[:, :patch]

    given = pltpu.make_async_remote_copy(
        src_ref=result, dst_ref=handed, send_sem=send_r, recv_sem=recv_r,
        device_id=partner, device_id_type=MESH,
    )

    def row_copy(by, t, to):
        return pltpu.make_async_remote_copy(
            src_ref=low, dst_ref=tokens.at[2 - by],
            send_sem=send_h.at[2 - by, t], recv_sem=recv_h.at[2 - by],
            device_id={"section": t, "seq": lax.rem(to + devices, devices)}, device_id_type=MESH,
        )

    side_copy = pltpu.make_async_remote_copy(
        src_ref=low, dst_ref=tokens.at[2], send_sem=send_h.at[2, 0], recv_sem=recv_h.at[2],
        device_id=partner, device_id_type=MESH,
    )

    def inside(by):
        return jnp.logical_and(me + by >= 0, me + by < devices)

    def sent_all():
        @pl.loop(0, devices)
        def _(d):
            @pl.when(d != me)
            def _():
                for c in range(chunks):
                    q_copy(c, d, me).wait_send()
                    kv_copy(c, d, me).wait_send()

    @pl.when(last)
    def _():
        for c in range(chunks):
            if c == chunks - 1:
                sent_all()
                pl.semaphore_signal(go, inc=1, device_id=partner, device_id_type=MESH)
            attend(c)
        send_parts()
        settle()
        low[...] = resd[...].astype(BF16)
        for by in (1, -1, 2, -2):
            for t in range(sections):

                @pl.when(inside(by))
                def _():
                    row_copy(by, t, me + by).start()

        side_copy.start()
        given.start()
        tokens[2] = low[...]

    @pl.when(jnp.logical_not(last))
    def _():
        pl.semaphore_wait(go, 1)
        for c in range(chunks):

            @pl.loop(0, groups)
            def _(k):
                send(c, turn(k))

        side_copy.wait_recv()

    for by in (1, -1, 2, -2):

        @pl.when(inside(-by))
        def _():
            row_copy(by, 0, me - by).wait_recv()

    def moved(value, by):
        position = rows_of(value.shape)
        if by > 0:
            return jnp.where(position > 0, pltpu.roll(value, 1, 0), 0.0)
        return jnp.where(position < cols - 1, pltpu.roll(value, cols - 1, 0), 0.0)

    def put(buf, index, value):
        phases = value.shape[0]
        buf[index, 1 : phases + 1] = value.astype(BF16)
        buf[index, 0] = moved(value[phases - 1], 1).astype(BF16)
        buf[index, phases + 1] = moved(value[0], -1).astype(BF16)

    def act(value, gain):
        square = jnp.mean(value * value, axis=-1, keepdims=True)
        h = value * (0.5 * lax.rsqrt(square + norm_eps)) * gain[...]
        return h + h * jnp.tanh(h)

    def flat(value):
        return value.reshape(-1, value.shape[-1])

    cells = []
    for i in range(5):
        value = tokens[i].astype(F32)
        first = lanes_of(value.shape) < patch
        cells.append((
            jnp.where(first, moved(value, 1), value).astype(BF16),
            jnp.where(first, value, moved(value, -1)).astype(BF16),
        ))
    for a in (0, 1):
        for b in (0, 1):
            x = []
            for j in range(4):
                above, below = cells[j][b], cells[j + 1][b]
                if a == 0:
                    above = scaled(above, keep[j])
                else:
                    below = scaled(below, keep[j])
                x.append(jnp.concatenate([above, below], axis=1))
            y = dot(jnp.concatenate(x, axis=0), w_in[2 * a + b]).astype(BF16)
            for j in range(4):
                a1[2 * j + 1 - a, b] = y[j * cols : (j + 1) * cols]

    shift = section

    for i in range(7):
        put(p1, i, act(a1[i + shift].astype(F32), g1))

    mine[4].wait()
    given_w[4].wait_recv()
    outs1 = w_first.shape[1] // 2
    for n in range(2):
        taps = []
        for p in range(3):
            for q in range(3):
                piece = []
                for j in range(5):
                    value = p1[j + p, q : q + 2]
                    if p == 0:
                        value = scaled(value, keep[4 + j])
                    elif p == 2:
                        value = scaled(value, keep[5 + j])
                    piece.append(flat(value))
                taps.append(jnp.concatenate(piece, axis=0))
        lanes = slice(n * outs1, (n + 1) * outs1)
        y = dot(jnp.concatenate(taps, axis=1), w_first[:, lanes])
        for j in range(5):
            base = a1[j + 1 + shift, :, :, lanes]
            value = base.astype(F32) + y[2 * j * cols : 2 * (j + 1) * cols].reshape(base.shape)
            x1[j, 1:3, :, lanes] = value.astype(BF16)
            x1[j, 0, :, lanes] = moved(value[1], 1).astype(BF16)
            x1[j, 3, :, lanes] = moved(value[0], -1).astype(BF16)

    for k in range(4):
        a, b = k // 2, k % 2
        taps = []
        for p in (0, 1):
            for q in (0, 1):
                piece = []
                for j in range(4):
                    value = x1[j + p, b + q : b + q + 2]
                    piece.append(flat(scaled(value, keep[5 + j]) if a == p else value))
                taps.append(jnp.concatenate(piece, axis=0))
        y = dot(jnp.concatenate(taps, axis=1), w_up2[k]).astype(BF16)
        for j in range(4):
            for f in (0, 1):
                at = (2 * j + f) * cols
                a2[2 * j + 1 - a, 2 * f + b] = y[at : at + cols]

    for i in range(8):
        put(p2, i, act(a2[i].astype(F32), g2))

    mine[5].wait()
    given_w[5].wait_recv()

    for t in range(3):
        taps = []
        for p in range(3):
            for q in range(3):
                piece = []
                for j in range(2):
                    value = p2[2 * t + j + p, q : q + 4]
                    if (p, j) == (0, 0):
                        value = scaled(value, keep[10 + t])
                    elif (p, j) == (2, 1):
                        value = scaled(value, keep[11 + t])
                    piece.append(flat(value))
                taps.append(jnp.concatenate(piece, axis=0))
        y = dot(jnp.concatenate(taps, axis=1), w_second[...])
        for j in range(2):
            base = a2[2 * t + 1 + j]
            put(x2, 2 * t + j,
                base.astype(F32) + y[4 * j * cols : 4 * (j + 1) * cols].reshape(base.shape))

    for a in range(2):
        taps = []
        for p in (0, 1):
            for q in range(3):
                piece = []
                for j in range(4):
                    value = x2[j + a + p, q : q + 4]
                    if a == p and j + a in (1, 3):
                        value = scaled(value, keep[14 + j + a])
                    piece.append(flat(value))
                taps.append(jnp.concatenate(piece, axis=0))
        y = dot(jnp.concatenate(taps, axis=1), w_up3[a]).astype(BF16)
        outs3 = a3.shape[-1]
        for j in range(4):
            for f in range(4):
                at = (4 * j + f) * cols
                for b in (0, 1):
                    a3[2 * j + a, 2 * f + b] = y[at : at + cols, b * outs3 : (b + 1) * outs3]

    for i in range(8):
        put(p3, i, act(a3[i].astype(F32), g3))

    @pl.when(jnp.logical_not(last))
    def _():
        for c in range(chunks):
            attend(c)
        send_parts()

    for t in range(3):
        taps = []
        for p in range(3):
            for q in range(4):
                piece = []
                for j in range(2):
                    for e in range(4):
                        value = p3[2 * t + j + p, 2 * e + q]
                        if t != 1 and (p, j) in ((2, 0), (0, 1)):
                            value = scaled(value, keep[21 + t])
                        piece.append(value)
                taps.append(jnp.concatenate(piece, axis=0))
        y = dot(jnp.concatenate(taps, axis=1), w_third[...])
        outs3 = a3.shape[-1]
        for j in range(2):
            value = jnp.stack([
                y[(4 * j + f // 2) * cols : (4 * j + f // 2 + 1) * cols,
                  (f % 2) * outs3 : (f % 2 + 1) * outs3]
                for f in range(8)
            ])
            value = (a3[2 * t + 1 + j].astype(F32) + value).astype(BF16).astype(F32)
            put(p4, 2 * t + j, act(value, g4))

    p4[0] = scaled(p4[0], keep[21])
    p4[5] = scaled(p4[5], keep[23])
    window = jnp.concatenate(
        [
            jnp.concatenate([p4[s + r, at] for s in range(4)], axis=0)
            for r in range(3)
            for at in range(10)
        ],
        axis=1,
    )
    colors = lax.dot_general(w_color[...], window, NT, preferred_element_type=F32)
    lines = []
    for s in range(4):
        line = []
        for pair in range(4):
            lanes = slice((s // 2) * 128, (s // 2 + 1) * 128)
            even = colors[16 * pair : 16 * pair + 8, lanes]
            odd = colors[16 * pair + 8 : 16 * pair + 16, lanes]
            first = lanes_of(even.shape) < cols
            if s % 2 == 0:
                line.append(jnp.where(first, even, swap_halves(odd)))
            else:
                line.append(jnp.where(first, swap_halves(even), odd))
        lines.append(jnp.concatenate(line, axis=1))
    value = jnp.concatenate(lines, axis=0)
    high = value.astype(BF16)
    rest = value - high.astype(F32)
    middle = rest.astype(BF16)
    final = (rest - middle.astype(F32)).astype(BF16)
    placed = dot(jnp.concatenate([high, middle, final], axis=0), order[...])
    placed = placed[:32] + (placed[32:64] + placed[64:])
    for k in range(picture.shape[0]):
        for s in range(4):
            picture[k, s : s + 1] = placed[8 * s + k : 8 * s + k + 1]

    shown = pltpu.make_async_copy(picture, image.at[section], out_sem)
    shared = pltpu.make_async_remote_copy(
        src_ref=picture, dst_ref=image.at[section], send_sem=send_i, recv_sem=recv_i,
        device_id=partner, device_id_type=MESH,
    )
    shared.start()
    shown.start()

    @pl.when(jnp.logical_not(last))
    def _():
        settle()
        given.start()

    given.wait_recv()
    given.wait_send()

    @pl.when(last)
    def _():
        side_copy.wait_send()
        for by in (1, -1, 2, -2):
            for t in range(sections):

                @pl.when(inside(by))
                def _():
                    row_copy(by, t, me + by).wait_send()

    @pl.when(jnp.logical_not(last))
    def _():
        sent_all()

    @pl.loop(0, devices)
    def _(d):
        @pl.when(d != me)
        def _():
            part_copy(d, me).wait_send()

    for copy in given_w:
        copy.wait_send()
    shown.wait()
    shared.wait()


def finish_kernel(handed, image, handed_out, image_out):
    handed_out[...] = handed[...]
    for s in range(2):
        image_out[:, 4 * s : 4 * s + 4] = image[s]


def body(
    latents, cond, embed, audio_table, audio_map, out_proj, tile_start,
    conv_input, conv_first, conv_second_up, conv_second, conv_third_up, conv_third, conv_color,
    gain_first, gain_second, gain_third, gain_color,
):
    devices, sections = lax.axis_size("seq"), lax.axis_size("section")
    splits = max(devices // HEADS, 1)
    per = max(HEADS // devices, 1)
    groups = devices // splits
    chunk = 2 if per % 2 == 0 else 1
    chunks = per // chunk
    wide = chunk * HSIZE
    latent = latents[0]
    count, patch = latent.shape
    half = count // splits
    features = cond.shape[-1]
    depth = -(-(patch + audio_table.shape[1]) // 128) * 128
    flat = lambda w: w.reshape(-1, w.shape[-1])
    taps = lambda w: w.reshape(9, *w.shape[2:])
    turned = lambda w: taps(jnp.swapaxes(w, 2, 3))
    c1, c2 = 2 * conv_first.shape[3], 2 * conv_second.shape[3]
    c3 = 2 * conv_third.shape[3]
    rgb = conv_color.shape[3]
    vmem = lambda shape, kind=BF16: pltpu.VMEM(shape, kind)
    dma = pltpu.SemaphoreType.DMA
    hbm = pl.BlockSpec(memory_space=pl.ANY)
    smem = pl.BlockSpec(memory_space=pltpu.SMEM)
    whole = pl.BlockSpec(memory_space=pltpu.VMEM)
    operands = (
        audio_map, tile_start,
        latent, cond[0], embed[0], audio_table[0], out_proj[0].T,
        flat(conv_input), flat(conv_first), taps(conv_second_up), flat(conv_second),
        turned(conv_third_up), turned(conv_third), flat(conv_color).T,
        gain_first[None], gain_second[None], gain_third[None], gain_color[None],
    )
    handed, image = pl.pallas_call(
        functools.partial(step_kernel, splits, per, chunk, sections, devices),
        out_shape=(
            jax.ShapeDtypeStruct(latent.shape, F32),
            jax.ShapeDtypeStruct((2, rgb, 4, 8 * count), F32),
        ),
        in_specs=[smem] * 2 + [hbm] * (len(operands) - 2),
        out_specs=(whole, whole),
        scratch_shapes=[
            vmem((count, patch), F32), vmem((count, 2 * patch), F32), vmem((count, depth)),
            vmem((3, count, features)), vmem((depth, features)), vmem((patch, features)),
            vmem((depth, features)), vmem((patch, features)),
            vmem((groups, chunks, count, wide)), vmem((groups, chunks, count, wide + 128)),
            vmem((chunks, devices * half, wide)), vmem((chunks, devices * count, wide + 128)),
            vmem((devices * half, 128), F32),
            vmem((devices, half // 2, 128), F32), vmem((devices, half // 2, 128), F32),
            vmem((count, 2 * patch), F32), vmem((count, patch), F32),
            vmem((count, 2 * patch)), vmem((5, count, 2 * patch)),
            pltpu.SMEM((24,), F32),
            vmem((9 * patch // 4, c1)), vmem((9 * c1, c1)), vmem((9, c1, c2)),
            vmem((9 * c2, c2)), vmem((9, c3, c2)), vmem((9, c3, c3)), vmem((rgb, 9 * c3)),
            vmem((1, c1), F32), vmem((1, c2), F32), vmem((1, c3), F32), vmem((1, c3), F32),
            vmem((4, 4 * patch, c1)), vmem((4, 4 * c1, c2)), vmem((2, 6 * c2, 2 * c3)),
            vmem((12 * c3, 2 * c3)), vmem((64, 30 * c3)), vmem((8 * count, 8 * count)),
            vmem((8, 2, count, c1)), vmem((7, 4, count, c1)), vmem((5, 4, count, c1)),
            vmem((8, 4, count, c2)), vmem((8, 6, count, c2)), vmem((6, 6, count, c2)),
            vmem((8, 8, count, c3)), vmem((8, 10, count, c3)), vmem((6, 10, count, c3)),
            vmem((rgb, 4, 8 * count), F32),
            dma((13,)), dma((chunks, devices)), dma((chunks, devices)),
            dma((chunks, devices)), dma((chunks, devices)), dma((chunks, 2)),
            dma((devices,)), dma((devices,)), dma((6,)), dma((6,)), dma((6,)),
            dma((5, sections)), dma((5,)), dma, dma, dma, dma, dma,
            pltpu.SemaphoreType.REGULAR,
        ],
        compiler_params=pltpu.CompilerParams(
            collective_id=0, has_side_effects=True, vmem_limit_bytes=60 * 1024 * 1024
        ),
    )(*operands)
    handed, image = pl.pallas_call(
        finish_kernel,
        out_shape=(
            jax.ShapeDtypeStruct(latent.shape, F32),
            jax.ShapeDtypeStruct((rgb, 8, 8 * count), F32),
        ),
        in_specs=[whole, whole],
        out_specs=(whole, whole),
    )(handed, image)
    return (handed[None], image)


def solution(mesh):
    in_specs = (
        P("section", ("replica", "seq"), None),
        P("section", None, ("replica", "seq"), None),
        P("section", None, None, None),
        P("section", "replica", None),
        P(("replica", "seq")),
        P("section", None, None),
        P("replica"),
        P(None, None, None, "section"),
        P(None, None, None, "section"),
        P(None, None, None, "section"),
        P(None, None, None, "section"),
        P(None, None, None, "section"),
        P(None, None, None, "section"),
        P(),
        P(),
        P(),
        P(),
        P(),
    )
    out_specs = (P("section", ("replica", "seq"), None), P(None, ("replica", "seq"), None))
    return jax.shard_map(body, mesh=mesh, in_specs=in_specs, out_specs=out_specs, check_vma=False)
```

```python
import functools
import math

import jax
import jax.numpy as jnp
from jax import lax
from jax.experimental import pallas as pl
from jax.experimental.pallas import tpu as pltpu
from jax.sharding import PartitionSpec as P

HEADS = 32
HSIZE = 128


step_size = -0.5
norm_eps = 1e-06


MESH = pl.DeviceIdType.MESH
F32, BF16 = jnp.float32, jnp.bfloat16
NT = (((1,), (1,)), ((), ()))


def lanes_of(shape):
    return lax.broadcasted_iota(jnp.int32, shape, len(shape) - 1)


def rows_of(shape):
    return lax.broadcasted_iota(jnp.int32, shape, len(shape) - 2)


def swap_halves(value):
    return pltpu.roll(value, value.shape[1] // 2, 1)


def dot(x, w):
    return jnp.dot(x, w, preferred_element_type=F32)


def scaled(value, factor):
    return value * lax.broadcast(factor, value.shape).astype(BF16)


def pairs(x, y, z):
    return ((x, y + z), (x + y, z))


def lift_second(raw, lifted):
    depth = raw.shape[1]
    chunk = 64

    @pl.loop(0, depth // chunk)
    def _(i):
        row = pl.multiple_of(i * chunk, chunk)
        w = [raw[t, pl.ds(row, chunk)].astype(F32) for t in range(9)]
        by_row = [pairs(w[q], w[3 + q], w[6 + q]) for q in range(3)]
        for a in (0, 1):
            for p in (0, 1):
                cols = pairs(*(by_row[q][a][p] for q in range(3)))
                for b in (0, 1):
                    for q in (0, 1):
                        at = pl.multiple_of((2 * p + q) * depth + row, chunk)
                        lifted[2 * a + b, pl.ds(at, chunk)] = cols[b][q].astype(BF16)


def lift_third_up(raw, lifted):
    outs, depth = raw.shape[1:]
    zero = jnp.zeros((depth, outs), BF16)
    w = [raw[t].astype(F32) for t in range(9)]
    by_row = [pairs(w[q], w[3 + q], w[6 + q]) for q in range(3)]
    for a in (0, 1):
        for p in (0, 1):
            cols = pairs(*(by_row[q][a][p] for q in range(3)))
            for b in (0, 1):
                for at in range(3):
                    inside = 0 <= at - b <= 1
                    block = cols[b][at - b].T.astype(BF16) if inside else zero
                    row = (3 * p + at) * depth
                    lifted[a, row : row + depth, b * outs : (b + 1) * outs] = block


def lift_third(raw, lifted):
    outs, depth = raw.shape[1:]
    zero = jnp.zeros((depth, outs), BF16)
    for r in range(3):
        for at in range(4):
            for e in (0, 1):
                inside = 0 <= at - e <= 2
                block = raw[3 * r + at - e].astype(F32).T.astype(BF16) if inside else zero
                row = (4 * r + at) * depth
                lifted[row : row + depth, e * outs : (e + 1) * outs] = block


def lift_input(raw, lifted, cell):
    chans = cell // 4
    zero = jnp.zeros((chans, raw.shape[1]), BF16)
    for a in (0, 1):
        for b in (0, 1):
            blocks = []
            for p in (0, 1):
                for q in (0, 1):
                    for i in (0, 1):
                        for j in (0, 1):
                            u, v = 2 * p + i - 1 + a, 2 * q + j - 1 + b
                            inside = 0 <= u <= 2 and 0 <= v <= 2
                            row = (3 * u + v) * chans
                            blocks.append(raw[row : row + chans] if inside else zero)
            lifted[2 * a + b] = jnp.concatenate(blocks, axis=0)


def lift_color(raw, lifted):
    color = raw[...].astype(F32)
    color = jnp.concatenate([color, jnp.zeros((8 - color.shape[0], color.shape[1]), F32)], axis=0)
    depth = color.shape[1] // 9
    zero = jnp.zeros((8, depth), F32)
    tile = lambda t: color[:, t * depth : (t + 1) * depth]
    for pair in range(4):
        blocks = []
        for f in (2 * pair, 2 * pair + 1):
            blocks.append(
                jnp.concatenate(
                    [
                        tile(3 * r + at - f) if 0 <= at - f <= 2 else zero
                        for r in range(3)
                        for at in range(10)
                    ],
                    axis=1,
                )
            )
        lifted[16 * pair : 16 * (pair + 1)] = jnp.concatenate(blocks, axis=0).astype(BF16)


def step_kernel(
    splits, per, chunk, sections, devices,
    amap, starts,
    latent, cond, embed, table, out_t,
    c_in, c_first, c_up2, c_second, c_up3, c_third, c_color, gain1, gain2, gain3, gain4,
    handed, image,
    lat, latd, xcat, condv, eq, ek, ev, wt, sq, skv, gq, gkv, acc, part, parts, resd, result,
    low, tokens, keep,
    r_in, w_first, r_up2, w_second, r_up3, r_third, r_color, g1, g2, g3, g4,
    w_in, w_up2, w_up3, w_third, w_color, order,
    a1, p1, x1, a2, p2, x2, a3, p3, p4, picture,
    in_sem, send_q, recv_q, send_kv, recv_kv, own_sem, send_p, recv_p,
    here_sem, send_w, recv_w, send_h, recv_h, send_r, recv_r, send_i, recv_i, out_sem, go,
):
    me = lax.axis_index("seq")
    section = lax.axis_index("section")
    last = section == sections - 1
    partner = {"section": lax.rem(section + 1, sections)}
    groups = devices // splits
    count, patch = lat.shape
    half = count // splits
    wide = chunk * HSIZE
    chunks = per // chunk
    my_group = me // splits
    cols = count

    tokens[...] = jnp.zeros(tokens.shape, BF16)
    barrier = pltpu.get_barrier_semaphore()
    for t in range(sections):
        peer = lax.rem(section + t, sections)

        @pl.loop(0 if t else 1, devices)
        def _(k):
            d = lax.rem(me + k, devices)
            pl.semaphore_signal(
                barrier, inc=1, device_id={"section": peer, "seq": d}, device_id_type=MESH
            )

    frames = table.shape[0]
    loads = [
        pltpu.make_async_copy(src, dst, in_sem.at[k])
        for k, (src, dst) in enumerate(
            (
                (latent, lat), (embed.at[0], eq.at[pl.ds(0, patch)]),
                (table, eq.at[pl.ds(patch, frames)]), (embed.at[2], ev.at[pl.ds(0, patch)]),
                (table, ev.at[pl.ds(patch, frames)]), (embed.at[1], ek), (cond, condv),
                (out_t, wt), (gain1, g1), (gain2, g2), (gain3, g3), (gain4, g4),
                (c_color, r_color),
            )
        )
    ]
    for copy in loads:
        copy.start()

    weights = ((c_third, r_third), (c_in, r_in), (c_up3, r_up3), (c_up2, r_up2),
               (c_first, w_first), (c_second, w_second))

    def half_of(dst, k):
        if k in (0, 2):
            size = dst.shape[1] // 2
            return dst.at[:, pl.ds(pl.multiple_of(section * size, size), size)]
        size = dst.shape[-1] // 2
        lanes = pl.ds(pl.multiple_of(section * size, size), size)
        return dst.at[:, :, lanes] if len(dst.shape) == 3 else dst.at[:, lanes]

    mine = [
        pltpu.make_async_copy(src, half_of(dst, k), here_sem.at[k])
        for k, (src, dst) in enumerate(weights)
    ]
    given_w = [
        pltpu.make_async_remote_copy(
            src_ref=src, dst_ref=half_of(dst, k), send_sem=send_w.at[k], recv_sem=recv_w.at[k],
            device_id=partner, device_id_type=MESH,
        )
        for k, (src, dst) in enumerate(weights)
    ]

    blocks = starts.shape[0]

    def joined(by):
        block = me + by
        inside = jnp.logical_and(block >= 0, block + 1 < blocks)
        begins = starts[jnp.clip(block + 1, 0, blocks - 1)]
        return jnp.where(jnp.logical_and(inside, begins == 0), 1.0, 0.0).astype(F32)

    k_a, k_b, k_c, k_d = (joined(by) for by in (-2, -1, 0, 1))
    one = jnp.float32(1.0)
    upper = section == 0
    either = lambda x, y: jnp.where(upper, x, y)
    level1 = [either(x, y) for x, y in (
        (k_a, one), (one, k_b), (k_b, one), (one, k_c), (k_c, one), (one, k_d))]
    level2 = [either(x, y) for x, y in ((one, k_b), (k_b, one), (one, k_c), (k_c, one))]
    b_or, c_or = either(k_b, one), either(one, k_c)
    for k, value in enumerate(
        [k_a, k_b, k_c, k_d] + level1 + level2 + [one, b_or, one, c_or, one, one, one]
        + [b_or, one, c_or]
    ):
        keep[k] = value

    zrow = patch + frames
    eq[zrow:] = jnp.zeros((eq.shape[0] - zrow, eq.shape[1]), BF16)
    ev[zrow:] = jnp.zeros((ev.shape[0] - zrow, ev.shape[1]), BF16)
    perm_row = rows_of(order.shape)
    perm_col = lanes_of(order.shape)
    phase = lax.div(perm_row, jnp.int32(cols))
    target = (perm_row - phase * cols) * 8 + phase
    order[...] = jnp.where(perm_col == target, 1.0, 0.0).astype(BF16)

    loads[0].wait()
    latd[:, :patch] = lat[...]
    latd[:, patch:] = lat[...]
    row = rows_of(xcat.shape)
    lane = lanes_of(xcat.shape)
    per_block = count // amap.shape[0]
    frame = lax.broadcast(amap[0], xcat.shape)
    for k in range(1, amap.shape[0]):
        frame = jnp.where(row >= k * per_block, amap[k], frame)
    padded = latd[...]
    if xcat.shape[1] > padded.shape[1]:
        extra = xcat.shape[1] - padded.shape[1]
        padded = jnp.concatenate([padded, jnp.zeros((count, extra), F32)], axis=1)
    onehot = jnp.where(lane == frame + patch, 1.0, 0.0)
    xcat[...] = jnp.where(lane < patch, padded, onehot).astype(BF16)
    for copy in loads[1:8]:
        copy.wait()

    def q_copy(c, d, src):
        return pltpu.make_async_remote_copy(
            src_ref=sq.at[d // splits, c, pl.ds(lax.rem(d, splits) * half, half)],
            dst_ref=gq.at[c, pl.ds(src * half, half)],
            send_sem=send_q.at[c, d], recv_sem=recv_q.at[c, src],
            device_id={"seq": d}, device_id_type=MESH,
        )

    def kv_copy(c, d, src):
        return pltpu.make_async_remote_copy(
            src_ref=skv.at[d // splits, c],
            dst_ref=gkv.at[c, pl.ds(src * count, count)],
            send_sem=send_kv.at[c, d], recv_sem=recv_kv.at[c, src],
            device_id={"seq": d}, device_id_type=MESH,
        )

    near = max(groups // 2, 1)
    quarter = max(groups // 4, 1)
    inner = lax.rem((my_group // quarter + 1) // 2, 2)

    def turn(k):
        side = lax.rem(my_group // near + inner + k // near, max(groups // near, 1))
        return side * near + lax.rem(my_group + 1 + lax.rem(k, near), near)

    sharp = math.log2(math.e) / math.sqrt(HSIZE)

    def send(c, g):
        @pl.loop(0, splits)
        def _(r):
            d = g * splits + r

            @pl.when(d != me)
            def _():
                q_copy(c, d, me).start()
                kv_copy(c, d, me).start()

    pl.semaphore_wait(barrier, sections * devices - 1)
    for copy in given_w[:2]:
        copy.start()
    for copy in mine:
        copy.start()

    for c in range(chunks):

        @pl.loop(0, groups)
        def _(k):
            g = turn(k)
            at = pl.ds(pl.multiple_of(g * (per * HSIZE) + c * wide, HSIZE), wide)
            q = dot(xcat[...], eq[:, at]) + condv[0, :, at].astype(F32)
            key = dot(xcat[:, :patch], ek[:, at]) + condv[1, :, at].astype(F32)
            v = dot(xcat[...], ev[:, at]) + condv[2, :, at].astype(F32)
            w = wt[:, at]
            if chunk == 2:
                first = lanes_of(w.shape) < HSIZE
                zero = jnp.zeros(w.shape, BF16)
                w = jnp.concatenate([jnp.where(first, w, zero), jnp.where(first, zero, w)], axis=0)
            else:
                w = jnp.concatenate([w, jnp.zeros((128 - w.shape[0], w.shape[1]), BF16)], axis=0)
            mixed = lax.dot_general(v.astype(BF16), w, NT, preferred_element_type=F32)
            sq[g, c] = q.astype(BF16)
            skv[g, c, :, :wide] = key.astype(BF16)
            skv[g, c, :, wide:] = mixed.astype(BF16)

            @pl.when(last)
            def _():
                send(c, g)

    for copy in given_w[2:]:
        copy.start()

    own = []
    for c in range(chunks):
        own.append(pltpu.make_async_copy(
            sq.at[my_group, c, pl.ds(lax.rem(me, splits) * half, half)],
            gq.at[c, pl.ds(me * half, half)], own_sem.at[c, 0],
        ))
        own.append(pltpu.make_async_copy(
            skv.at[my_group, c], gkv.at[c, pl.ds(me * count, count)], own_sem.at[c, 1]
        ))
    for copy in own:
        copy.start()

    for copy in loads[8:]:
        copy.wait()
    lift_color(r_color, w_color)
    mine[0].wait()
    given_w[0].wait_recv()
    lift_third(r_third, w_third)
    mine[1].wait()
    given_w[1].wait_recv()
    lift_input(r_in, w_in, patch)
    mine[2].wait()
    given_w[2].wait_recv()
    lift_third_up(r_up3, w_up3)
    mine[3].wait()
    given_w[3].wait_recv()
    lift_second(r_up2, w_up2)

    queries = gq.shape[1]
    block = min(256, queries)
    parts_of = queries // block
    lane128 = lanes_of((block, 128))
    both = half // 2

    def attend(c):
        own[2 * c].wait()
        own[2 * c + 1].wait()

        @pl.loop(0, devices)
        def _(d):
            @pl.when(d != me)
            def _():
                q_copy(c, d, d).wait_recv()
                kv_copy(c, d, d).wait_recv()

        @pl.loop(0, parts_of)
        def _(i):
            at = pl.ds(pl.multiple_of(i * block, block), block)
            outs = []
            for h in range(chunk):
                own_lanes = slice(h * HSIZE, (h + 1) * HSIZE)
                scores = lax.dot_general(
                    gq[c, at, own_lanes], gkv[c, :, own_lanes], NT, preferred_element_type=F32
                ) * sharp
                top = jnp.max(scores, axis=1, keepdims=True)
                values = gkv[c, :, wide:]
                values = jnp.concatenate([values, jnp.ones(values.shape, BF16)], axis=1)
                summed = dot(jnp.exp2(scores - top).astype(BF16), values)
                outs.append(summed[:, :128] / summed[:, 128:])
            value = outs[0] if chunk == 1 else jnp.where(lane128 < patch, outs[0], outs[1])
            if c > 0:
                value = value + acc[at]
            if c < chunks - 1:
                acc[at] = value
            else:
                value = value + swap_halves(value)
                for k in range(block // half):
                    low_rows = value[k * half : k * half + both]
                    high_rows = value[k * half + both : (k + 1) * half]
                    first = lanes_of(low_rows.shape) < patch
                    part[i * (block // half) + k] = jnp.where(first, low_rows, high_rows)

    def part_copy(d, src):
        return pltpu.make_async_remote_copy(
            src_ref=part.at[d], dst_ref=parts.at[src],
            send_sem=send_p.at[d], recv_sem=recv_p.at[src],
            device_id={"seq": d}, device_id_type=MESH,
        )

    def send_parts():
        @pl.loop(1, devices)
        def _(k):
            part_copy(lax.rem(me + k, devices), me).start()

    def settle():
        @pl.loop(0, devices)
        def _(d):
            @pl.when(d != me)
            def _():
                part_copy(d, d).wait_recv()

        for r in range(splits):
            total = jnp.zeros((both, 128), F32)
            for g in range(groups):
                d = g * splits + r
                total = total + jnp.where(d == me, part[d], parts[d])
            first = lanes_of(total.shape) < patch
            other = swap_halves(total)
            at = r * half
            low_rows = jnp.where(first, total, other)
            high_rows = jnp.where(first, other, total)
            resd[at : at + both] = latd[at : at + both] + step_size * low_rows
            resd[at + both : at + half] = latd[at + both : at + half] + step_size * high_rows
        result[...] = resd[:, :patch]

    given = pltpu.make_async_remote_copy(
        src_ref=result, dst_ref=handed, send_sem=send_r, recv_sem=recv_r,
        device_id=partner, device_id_type=MESH,
    )

    def row_copy(by, t, to):
        return pltpu.make_async_remote_copy(
            src_ref=low, dst_ref=tokens.at[2 - by],
            send_sem=send_h.at[2 - by, t], recv_sem=recv_h.at[2 - by],
            device_id={"section": t, "seq": lax.rem(to + devices, devices)}, device_id_type=MESH,
        )

    side_copy = pltpu.make_async_remote_copy(
        src_ref=low, dst_ref=tokens.at[2], send_sem=send_h.at[2, 0], recv_sem=recv_h.at[2],
        device_id=partner, device_id_type=MESH,
    )

    def inside(by):
        return jnp.logical_and(me + by >= 0, me + by < devices)

    def sent_all():
        @pl.loop(0, devices)
        def _(d):
            @pl.when(d != me)
            def _():
                for c in range(chunks):
                    q_copy(c, d, me).wait_send()
                    kv_copy(c, d, me).wait_send()

    @pl.when(last)
    def _():
        for c in range(chunks):
            if c == chunks - 1:
                sent_all()
                pl.semaphore_signal(go, inc=1, device_id=partner, device_id_type=MESH)
            attend(c)
        send_parts()
        settle()
        low[...] = resd[...].astype(BF16)
        for by in (1, -1, 2, -2):
            for t in range(sections):

                @pl.when(inside(by))
                def _():
                    row_copy(by, t, me + by).start()

        side_copy.start()
        given.start()
        tokens[2] = low[...]

    @pl.when(jnp.logical_not(last))
    def _():
        pl.semaphore_wait(go, 1)
        for c in range(chunks):

            @pl.loop(0, groups)
            def _(k):
                send(c, turn(k))

        side_copy.wait_recv()

    for by in (1, -1, 2, -2):

        @pl.when(inside(-by))
        def _():
            row_copy(by, 0, me - by).wait_recv()

    def moved(value, by):
        position = rows_of(value.shape)
        if by > 0:
            return jnp.where(position > 0, pltpu.roll(value, 1, 0), 0.0)
        return jnp.where(position < cols - 1, pltpu.roll(value, cols - 1, 0), 0.0)

    def put(buf, index, value):
        phases = value.shape[0]
        buf[index, 1 : phases + 1] = value.astype(BF16)
        buf[index, 0] = moved(value[phases - 1], 1).astype(BF16)
        buf[index, phases + 1] = moved(value[0], -1).astype(BF16)

    def act(value, gain):
        square = jnp.mean(value * value, axis=-1, keepdims=True)
        h = value * (0.5 * lax.rsqrt(square + norm_eps)) * gain[...]
        return h + h * jnp.tanh(h)

    def flat(value):
        return value.reshape(-1, value.shape[-1])

    cells = []
    for i in range(5):
        value = tokens[i].astype(F32)
        first = lanes_of(value.shape) < patch
        cells.append((
            jnp.where(first, moved(value, 1), value).astype(BF16),
            jnp.where(first, value, moved(value, -1)).astype(BF16),
        ))
    for a in (0, 1):
        for b in (0, 1):
            x = []
            for j in range(4):
                above, below = cells[j][b], cells[j + 1][b]
                if a == 0:
                    above = scaled(above, keep[j])
                else:
                    below = scaled(below, keep[j])
                x.append(jnp.concatenate([above, below], axis=1))
            y = dot(jnp.concatenate(x, axis=0), w_in[2 * a + b]).astype(BF16)
            for j in range(4):
                a1[2 * j + 1 - a, b] = y[j * cols : (j + 1) * cols]

    shift = section

    for i in range(7):
        put(p1, i, act(a1[i + shift].astype(F32), g1))

    mine[4].wait()
    given_w[4].wait_recv()
    outs1 = w_first.shape[1] // 2
    for n in range(2):
        taps = []
        for p in range(3):
            for q in range(3):
                piece = []
                for j in range(5):
                    value = p1[j + p, q : q + 2]
                    if p == 0:
                        value = scaled(value, keep[4 + j])
                    elif p == 2:
                        value = scaled(value, keep[5 + j])
                    piece.append(flat(value))
                taps.append(jnp.concatenate(piece, axis=0))
        lanes = slice(n * outs1, (n + 1) * outs1)
        y = dot(jnp.concatenate(taps, axis=1), w_first[:, lanes])
        for j in range(5):
            base = a1[j + 1 + shift, :, :, lanes]
            value = base.astype(F32) + y[2 * j * cols : 2 * (j + 1) * cols].reshape(base.shape)
            x1[j, 1:3, :, lanes] = value.astype(BF16)
            x1[j, 0, :, lanes] = moved(value[1], 1).astype(BF16)
            x1[j, 3, :, lanes] = moved(value[0], -1).astype(BF16)

    for k in range(4):
        a, b = k // 2, k % 2
        taps = []
        for p in (0, 1):
            for q in (0, 1):
                piece = []
                for j in range(4):
                    value = x1[j + p, b + q : b + q + 2]
                    piece.append(flat(scaled(value, keep[5 + j]) if a == p else value))
                taps.append(jnp.concatenate(piece, axis=0))
        y = dot(jnp.concatenate(taps, axis=1), w_up2[k]).astype(BF16)
        for j in range(4):
            for f in (0, 1):
                at = (2 * j + f) * cols
                a2[2 * j + 1 - a, 2 * f + b] = y[at : at + cols]

    for i in range(8):
        put(p2, i, act(a2[i].astype(F32), g2))

    mine[5].wait()
    given_w[5].wait_recv()

    for t in range(3):
        taps = []
        for p in range(3):
            for q in range(3):
                piece = []
                for j in range(2):
                    value = p2[2 * t + j + p, q : q + 4]
                    if (p, j) == (0, 0):
                        value = scaled(value, keep[10 + t])
                    elif (p, j) == (2, 1):
                        value = scaled(value, keep[11 + t])
                    piece.append(flat(value))
                taps.append(jnp.concatenate(piece, axis=0))
        y = dot(jnp.concatenate(taps, axis=1), w_second[...])
        for j in range(2):
            base = a2[2 * t + 1 + j]
            put(x2, 2 * t + j,
                base.astype(F32) + y[4 * j * cols : 4 * (j + 1) * cols].reshape(base.shape))

    for a in range(2):
        taps = []
        for p in (0, 1):
            for q in range(3):
                piece = []
                for j in range(4):
                    value = x2[j + a + p, q : q + 4]
                    if a == p and j + a in (1, 3):
                        value = scaled(value, keep[14 + j + a])
                    piece.append(flat(value))
                taps.append(jnp.concatenate(piece, axis=0))
        y = dot(jnp.concatenate(taps, axis=1), w_up3[a]).astype(BF16)
        outs3 = a3.shape[-1]
        for j in range(4):
            for f in range(4):
                at = (4 * j + f) * cols
                for b in (0, 1):
                    a3[2 * j + a, 2 * f + b] = y[at : at + cols, b * outs3 : (b + 1) * outs3]

    for i in range(8):
        put(p3, i, act(a3[i].astype(F32), g3))

    @pl.when(jnp.logical_not(last))
    def _():
        for c in range(chunks - 1):
            attend(c)

    for t in range(3):
        taps = []
        for p in range(3):
            for q in range(4):
                piece = []
                for j in range(2):
                    for e in range(4):
                        value = p3[2 * t + j + p, 2 * e + q]
                        if t != 1 and (p, j) in ((2, 0), (0, 1)):
                            value = scaled(value, keep[21 + t])
                        piece.append(value)
                taps.append(jnp.concatenate(piece, axis=0))
        y = dot(jnp.concatenate(taps, axis=1), w_third[...])
        outs3 = a3.shape[-1]
        for j in range(2):
            value = jnp.stack([
                y[(4 * j + f // 2) * cols : (4 * j + f // 2 + 1) * cols,
                  (f % 2) * outs3 : (f % 2 + 1) * outs3]
                for f in range(8)
            ])
            value = (a3[2 * t + 1 + j].astype(F32) + value).astype(BF16).astype(F32)
            put(p4, 2 * t + j, act(value, g4))

    @pl.when(jnp.logical_not(last))
    def _():
        attend(chunks - 1)
        send_parts()

    p4[0] = scaled(p4[0], keep[21])
    p4[5] = scaled(p4[5], keep[23])
    window = jnp.concatenate(
        [
            jnp.concatenate([p4[s + r, at] for s in range(4)], axis=0)
            for r in range(3)
            for at in range(10)
        ],
        axis=1,
    )
    colors = lax.dot_general(w_color[...], window, NT, preferred_element_type=F32)
    lines = []
    for s in range(4):
        line = []
        for pair in range(4):
            lanes = slice((s // 2) * 128, (s // 2 + 1) * 128)
            even = colors[16 * pair : 16 * pair + 8, lanes]
            odd = colors[16 * pair + 8 : 16 * pair + 16, lanes]
            first = lanes_of(even.shape) < cols
            if s % 2 == 0:
                line.append(jnp.where(first, even, swap_halves(odd)))
            else:
                line.append(jnp.where(first, swap_halves(even), odd))
        lines.append(jnp.concatenate(line, axis=1))
    value = jnp.concatenate(lines, axis=0)
    high = value.astype(BF16)
    rest = value - high.astype(F32)
    middle = rest.astype(BF16)
    final = (rest - middle.astype(F32)).astype(BF16)
    placed = dot(jnp.concatenate([high, middle, final], axis=0), order[...])
    placed = placed[:32] + (placed[32:64] + placed[64:])
    for k in range(picture.shape[0]):
        for s in range(4):
            picture[k, s : s + 1] = placed[8 * s + k : 8 * s + k + 1]

    shown = pltpu.make_async_copy(picture, image.at[section], out_sem)
    shared = pltpu.make_async_remote_copy(
        src_ref=picture, dst_ref=image.at[section], send_sem=send_i, recv_sem=recv_i,
        device_id=partner, device_id_type=MESH,
    )
    shared.start()
    shown.start()

    @pl.when(jnp.logical_not(last))
    def _():
        settle()
        given.start()

    given.wait_recv()
    given.wait_send()

    @pl.when(last)
    def _():
        side_copy.wait_send()
        for by in (1, -1, 2, -2):
            for t in range(sections):

                @pl.when(inside(by))
                def _():
                    row_copy(by, t, me + by).wait_send()

    @pl.when(jnp.logical_not(last))
    def _():
        sent_all()

    @pl.loop(0, devices)
    def _(d):
        @pl.when(d != me)
        def _():
            part_copy(d, me).wait_send()

    for copy in given_w:
        copy.wait_send()
    shown.wait()
    shared.wait()


def finish_kernel(handed, image, handed_out, image_out):
    handed_out[...] = handed[...]
    for s in range(2):
        image_out[:, 4 * s : 4 * s + 4] = image[s]


def body(
    latents, cond, embed, audio_table, audio_map, out_proj, tile_start,
    conv_input, conv_first, conv_second_up, conv_second, conv_third_up, conv_third, conv_color,
    gain_first, gain_second, gain_third, gain_color,
):
    devices, sections = lax.axis_size("seq"), lax.axis_size("section")
    splits = max(devices // HEADS, 1)
    per = max(HEADS // devices, 1)
    groups = devices // splits
    chunk = 2 if per % 2 == 0 else 1
    chunks = per // chunk
    wide = chunk * HSIZE
    latent = latents[0]
    count, patch = latent.shape
    half = count // splits
    features = cond.shape[-1]
    depth = -(-(patch + audio_table.shape[1]) // 128) * 128
    flat = lambda w: w.reshape(-1, w.shape[-1])
    taps = lambda w: w.reshape(9, *w.shape[2:])
    turned = lambda w: taps(jnp.swapaxes(w, 2, 3))
    c1, c2 = 2 * conv_first.shape[3], 2 * conv_second.shape[3]
    c3 = 2 * conv_third.shape[3]
    rgb = conv_color.shape[3]
    vmem = lambda shape, kind=BF16: pltpu.VMEM(shape, kind)
    dma = pltpu.SemaphoreType.DMA
    hbm = pl.BlockSpec(memory_space=pl.ANY)
    smem = pl.BlockSpec(memory_space=pltpu.SMEM)
    whole = pl.BlockSpec(memory_space=pltpu.VMEM)
    operands = (
        audio_map, tile_start,
        latent, cond[0], embed[0], audio_table[0], out_proj[0].T,
        flat(conv_input), flat(conv_first), taps(conv_second_up), flat(conv_second),
        turned(conv_third_up), turned(conv_third), flat(conv_color).T,
        gain_first[None], gain_second[None], gain_third[None], gain_color[None],
    )
    handed, image = pl.pallas_call(
        functools.partial(step_kernel, splits, per, chunk, sections, devices),
        out_shape=(
            jax.ShapeDtypeStruct(latent.shape, F32),
            jax.ShapeDtypeStruct((2, rgb, 4, 8 * count), F32),
        ),
        in_specs=[smem] * 2 + [hbm] * (len(operands) - 2),
        out_specs=(whole, whole),
        scratch_shapes=[
            vmem((count, patch), F32), vmem((count, 2 * patch), F32), vmem((count, depth)),
            vmem((3, count, features)), vmem((depth, features)), vmem((patch, features)),
            vmem((depth, features)), vmem((patch, features)),
            vmem((groups, chunks, count, wide)), vmem((groups, chunks, count, wide + 128)),
            vmem((chunks, devices * half, wide)), vmem((chunks, devices * count, wide + 128)),
            vmem((devices * half, 128), F32),
            vmem((devices, half // 2, 128), F32), vmem((devices, half // 2, 128), F32),
            vmem((count, 2 * patch), F32), vmem((count, patch), F32),
            vmem((count, 2 * patch)), vmem((5, count, 2 * patch)),
            pltpu.SMEM((24,), F32),
            vmem((9 * patch // 4, c1)), vmem((9 * c1, c1)), vmem((9, c1, c2)),
            vmem((9 * c2, c2)), vmem((9, c3, c2)), vmem((9, c3, c3)), vmem((rgb, 9 * c3)),
            vmem((1, c1), F32), vmem((1, c2), F32), vmem((1, c3), F32), vmem((1, c3), F32),
            vmem((4, 4 * patch, c1)), vmem((4, 4 * c1, c2)), vmem((2, 6 * c2, 2 * c3)),
            vmem((12 * c3, 2 * c3)), vmem((64, 30 * c3)), vmem((8 * count, 8 * count)),
            vmem((8, 2, count, c1)), vmem((7, 4, count, c1)), vmem((5, 4, count, c1)),
            vmem((8, 4, count, c2)), vmem((8, 6, count, c2)), vmem((6, 6, count, c2)),
            vmem((8, 8, count, c3)), vmem((8, 10, count, c3)), vmem((6, 10, count, c3)),
            vmem((rgb, 4, 8 * count), F32),
            dma((13,)), dma((chunks, devices)), dma((chunks, devices)),
            dma((chunks, devices)), dma((chunks, devices)), dma((chunks, 2)),
            dma((devices,)), dma((devices,)), dma((6,)), dma((6,)), dma((6,)),
            dma((5, sections)), dma((5,)), dma, dma, dma, dma, dma,
            pltpu.SemaphoreType.REGULAR,
        ],
        compiler_params=pltpu.CompilerParams(
            collective_id=0, has_side_effects=True, vmem_limit_bytes=60 * 1024 * 1024
        ),
    )(*operands)
    handed, image = pl.pallas_call(
        finish_kernel,
        out_shape=(
            jax.ShapeDtypeStruct(latent.shape, F32),
            jax.ShapeDtypeStruct((rgb, 8, 8 * count), F32),
        ),
        in_specs=[whole, whole],
        out_specs=(whole, whole),
    )(handed, image)
    return (handed[None], image)


def solution(mesh):
    in_specs = (
        P("section", ("replica", "seq"), None),
        P("section", None, ("replica", "seq"), None),
        P("section", None, None, None),
        P("section", "replica", None),
        P(("replica", "seq")),
        P("section", None, None),
        P("replica"),
        P(None, None, None, "section"),
        P(None, None, None, "section"),
        P(None, None, None, "section"),
        P(None, None, None, "section"),
        P(None, None, None, "section"),
        P(None, None, None, "section"),
        P(),
        P(),
        P(),
        P(),
        P(),
    )
    out_specs = (P("section", ("replica", "seq"), None), P(None, ("replica", "seq"), None))
    return jax.shard_map(body, mesh=mesh, in_specs=in_specs, out_specs=out_specs, check_vma=False)
```
